256 devices in a mesh: sub: 64 (over z, y, core), grp: 4 (over x).
Axes of the slice: x: 4, y: 4, z: 8, core: 2. Of those that a mesh axis runs over, the one named last changes fastest.
Arguments:
- coarse: float32 [6144, 128], P(('sub', 'grp')), may hold values from -6 to 6
- corner_idx: int32 [256, 24], P(('sub', 'grp')), may hold values from 0 to 6143, as said below
- coupling: bfloat16 [393216, 24], P(('sub', 'grp')), may hold values from -1.25 to 1.25
- force: bfloat16 [131072, 3, 128], P(('sub', 'grp')), may hold values from -6 to 6
- panel_inv: bfloat16 [1024, 384, 384], P(('sub', 'grp')), as said below
- panel_nodes: int32 [256, 4], P(('sub', 'grp')), may hold values from 64 to 128, as said below
- strain_disp: bfloat16 [6, 24, 32768], P(None, None, ('sub', 'grp')), may hold values from -1.25 to 1.25
- modulus: float32 [32768], P(('sub', 'grp')), may hold values from 0.5 to 4
- connect: int32 [8, 32768], P(None, ('sub', 'grp')), may hold values from 0 to 511, as said below
- interface: int32 [256, 224], P(('sub', 'grp')), may hold values from 0 to 511, as said below
- nodal_volume: float32 [131072], P(('sub', 'grp')), may hold values from 4 to 16
Outputs:
- displacement: bfloat16 [131072, 3, 128], P(('sub', 'grp'))
- nodal_stress: bfloat16 [131072, 6, 128], P(('sub', 'grp'))
The draws below stay inside these ranges and needn't reach their ends.
Inputs may be any that keep to these rules, and one draw needn't show every extreme that they name: `corner_idx`: the rows of subdomain (s, g) lie in the coarse blocks of subdomains (s', g') with |s' - s| <= 1 that exist, including blocks of all grp indices; they come in triples of consecutive rows. `panel_nodes`: every subdomain has one panel with exactly 128 live nodes and one with 64. `connect`: every entry is a live node of its subdomain (slot j < panel_nodes of its panel). `interface`: each row holds 224 distinct live nodes as eight lists: sub-lo (64), sub-hi (64), grp-lo (32), grp-hi (32), then edges ll, lh, hl, hh (8 each; first letter the sub side, second the grp side). Entry k of a list of (s, g) is the same physical node as entry k of the facing list of each neighbour: sub-hi with sub-lo of (s + 1, g), grp-hi with grp-lo of (s, g + 1); edge (x, y) with the edge of the neighbour across it that has the opposite letter on each side crossed. `panel_inv`: given inverses of the padded panels.
All inputs are finite; a program needn't handle non-finite values.
Results may differ from the reference program's by a relative error of at most 0.0058.
Values sent between devices are 32-bit elements; how exact they have to be, the bound alone decides.
A program may use at most 64 MiB of HBM per device.

```python
import math
import jax
import jax.numpy as jnp
import numpy as np
from jax import lax

PNODES = 128
PW = 384
NP = 4
NN = 512
NE = 128
NL = 128
NIS = 64
NIG = 32
NED = 8
NIF = 224
NCL = 24
CPD = 24
SUBDOMAINS = 256
NODES = 131072
DOFS = 393216
NELEMS = 32768
NCOARSE = 6144
N_SUB = 64
N_GRP = 4


def live_counts(key):
    base_key = jax.random.fold_in(key, 101)
    key_counts, key_full, key_empty = jax.random.split(base_key, 3)
    counts = jax.random.randint(key_counts, (SUBDOMAINS, NP), PNODES // 2, PNODES + 1)
    fullest = jax.random.randint(key_full, (SUBDOMAINS,), 0, NP)
    emptiest = (fullest + jax.random.randint(key_empty, (SUBDOMAINS,), 1, NP)) % NP
    panel_ids = jnp.arange(NP)[None, :]
    counts = jnp.where(panel_ids == fullest[:, None], PNODES, counts)
    counts = jnp.where(panel_ids == emptiest[:, None], PNODES // 2, counts)
    return counts.astype(jnp.int32)


def live_order(key):
    counts = live_counts(key)
    node_ids = jnp.arange(NN)
    live_mask = (node_ids % PNODES)[None, :] < jnp.take(counts, node_ids // PNODES, axis=1)
    row_keys = jax.random.split(jax.random.fold_in(key, 202), SUBDOMAINS)
    priority = jax.vmap(lambda k: jax.random.permutation(k, NN))(row_keys)
    priority = priority + jnp.where(live_mask, 0, NN)
    live_first = jnp.argsort(priority, axis=1).astype(jnp.int32)
    return (live_first, jnp.sum(counts, axis=1))


def draw_panel_nodes(key, part):
    return live_counts(key)


def draw_interface(key, part):
    live_first, total_live = live_order(key)
    return live_first[:, :NIF]


def draw_connect(key, part):
    live_first, total_live = live_order(key)
    picked = jax.random.randint(jax.random.fold_in(key, 303), (8, SUBDOMAINS, NE), 0, total_live[None, :, None])
    chosen = jnp.take_along_axis(jnp.broadcast_to(live_first[None], (8, SUBDOMAINS, NN)), picked, axis=2)
    return chosen.reshape(8, SUBDOMAINS * NE).astype(jnp.int32)


def draw_corner_idx(key, part):
    key_grp, key_step, key_node = jax.random.split(jax.random.fold_in(key, 404), 3)
    domain = jnp.arange(SUBDOMAINS)
    sub_pos = (domain // N_GRP)[:, None]
    grp_pos = (domain % N_GRP)[:, None]
    rand_grp = jax.random.randint(key_grp, (SUBDOMAINS, 8), 0, N_GRP)
    rand_step = jax.random.randint(key_step, (SUBDOMAINS, 8), -1, 2)
    node_pick = jax.random.randint(key_node, (SUBDOMAINS, 8), 0, CPD // 3)
    corner_slot = jnp.arange(8)[None, :]
    owner_sub = jnp.clip(sub_pos + rand_step, 0, N_SUB - 1)
    owner_sub = jnp.where(corner_slot == 0, jnp.maximum(sub_pos - 1, 0), owner_sub)
    owner_sub = jnp.where(corner_slot == 1, jnp.minimum(sub_pos + 1, N_SUB - 1), owner_sub)
    owner_sub = jnp.where((corner_slot >= 2) & (corner_slot <= 4), sub_pos, owner_sub)
    owner_grp = rand_grp
    owner_grp = jnp.where(corner_slot == 2, (grp_pos + 2) % N_GRP, owner_grp)
    owner_grp = jnp.where(corner_slot == 3, (grp_pos + 1) % N_GRP, owner_grp)
    owner_grp = jnp.where(corner_slot == 4, (grp_pos + N_GRP - 1) % N_GRP, owner_grp)
    first_dof = (owner_sub * N_GRP + owner_grp) * CPD + 3 * node_pick
    return (first_dof[:, :, None] + jnp.arange(3)[None, None, :]).reshape(SUBDOMAINS, NCL).astype(jnp.int32)


def draw_panel_inv(key, part):
    key_off, key_diag = jax.random.split(jax.random.fold_in(key, 505))
    full_shape = (SUBDOMAINS * NP, PW, PW)
    random_part = jnp.clip(jax.random.normal(key_off, full_shape, jnp.float32), -4.0, 4.0) * (0.5 / math.sqrt(PW))
    diag_part = jax.random.uniform(key_diag, (SUBDOMAINS * NP, PW), jnp.float32, 1.0, 3.0)
    return (random_part + jnp.eye(PW, dtype=jnp.float32)[None] * diag_part[:, None, :]).astype(jnp.bfloat16)


def block_scale(own_key, dims, cuts, least, high):
    factor_of = 1.0
    for position, shards_of in cuts:
        draws = jax.random.uniform(jax.random.fold_in(jax.random.fold_in(own_key, 6), position), (shards_of,), jnp.float32, least / len(cuts), high / len(cuts))
        factor_of = factor_of * jnp.repeat(jnp.exp(draws), dims[position] // shards_of).reshape((-1,) + (1,) * (len(dims) - 1 - position))
    return factor_of


def gaussian(rng, shape, spread, bound, cuts=(), kind=jnp.bfloat16):
    gain = block_scale(rng, shape, cuts, -0.22, 0.18) if cuts else 1.0
    array = jax.random.normal(rng, shape, jnp.float32) * spread * gain
    return jnp.minimum(jnp.maximum(array, -bound), bound).astype(kind)


def setup_inputs(seed: int = 0) -> dict:
    splits = jax.random.split(jax.random.key(seed), 12)
    return {
        "coarse": gaussian(splits[0], (NCOARSE, NL), 1.0, 6.0, ((0, 256),), jnp.float32),
        "corner_idx": draw_corner_idx(jax.random.fold_in(splits[11], 71), 0),
        "coupling": gaussian(splits[2], (DOFS, NCL), NCL ** -0.5, 1.25, ((0, 256),)),
        "force": gaussian(splits[3], (NODES, 3, NL), 1.0, 6.0, ((0, 256),)),
        "panel_inv": draw_panel_inv(jax.random.fold_in(splits[11], 71), 0),
        "panel_nodes": draw_panel_nodes(jax.random.fold_in(splits[11], 71), 0),
        "strain_disp": gaussian(splits[6], (6, 24, NELEMS), 24 ** -0.5, 1.25, ((2, 256),)),
        "modulus": jnp.clip(jnp.exp(math.log(4.0) - 2.0794415 * jax.random.uniform(splits[7], (NELEMS,), jnp.float32) ** block_scale(splits[7], (NELEMS,), ((0, 256),), -0.2, 0.2)), 0.5, 4.0),
        "connect": draw_connect(jax.random.fold_in(splits[11], 71), 0),
        "interface": draw_interface(jax.random.fold_in(splits[11], 71), 0),
        "nodal_volume": jnp.clip(jnp.exp(math.log(16.0) - 1.3862944 * jax.random.uniform(splits[10], (NODES,), jnp.float32) ** block_scale(splits[10], (NODES,), ((0, 256),), -0.2, 0.2)), 4.0, 16.0),
    }


POISSON = 0.3


def iso_matrix():
    lame_first = POISSON / ((1.0 + POISSON) * (1.0 - 2.0 * POISSON))
    shear_mod = 0.5 / (1.0 + POISSON)
    upper_block = jnp.full((3, 3), lame_first, jnp.float32) + jnp.eye(3, dtype=jnp.float32) * (2.0 * shear_mod)
    shear_block = jnp.eye(3, dtype=jnp.float32) * shear_mod
    zero_block = jnp.zeros((3, 3), jnp.float32)
    return jnp.concatenate([jnp.concatenate([upper_block, zero_block], 1), jnp.concatenate([zero_block, shear_block], 1)], 0)


def row_span(first_row, row_count):
    return np.arange(first_row, first_row + row_count)


def shifted(values, step_sub, step_grp):
    padding = [(1, 1), (1, 1)] + [(0, 0)] * (values.ndim - 2)
    padded = jnp.pad(values, padding)
    padded = lax.slice_in_dim(padded, 1 - step_sub, 1 - step_sub + N_SUB, axis=0)
    return lax.slice_in_dim(padded, 1 - step_grp, 1 - step_grp + N_GRP, axis=1)


def pick_rows(partial_rows, node_ids):
    return partial_rows[node_ids]


def put_rows(partial_rows, node_ids, new_rows):
    return partial_rows.at[node_ids].set(new_rows)


def reference(coarse, corner_idx, coupling, force, panel_inv, panel_nodes, strain_disp, modulus, connect, interface, nodal_volume):
    elastic = iso_matrix()
    corner_values = coarse[corner_idx]
    coupling_all = coupling.reshape(SUBDOMAINS, 3 * NN, NCL)
    force_all = force.reshape(SUBDOMAINS, 3 * NN, NL)
    inverse_all = panel_inv.reshape(SUBDOMAINS, NP, PW, PW)
    strain_all = jnp.moveaxis(strain_disp.reshape(6, 24, SUBDOMAINS, NE), 2, 0)
    modulus_all = modulus.reshape(SUBDOMAINS, NE)
    connect_all = jnp.moveaxis(connect.reshape(8, SUBDOMAINS, NE), 1, 0)

    def one_domain(pieces):
        values, coupled, load_rows, inverse, counts, strain_map, moduli, nodes_of = pieces
        correction = jnp.dot(coupled.astype(jnp.float32), values, precision=lax.Precision.HIGHEST)
        live_mask = jnp.arange(PW)[None, :] < 3 * counts[:, None]
        reduced = (load_rows.astype(jnp.float32) - correction).reshape(NP, PW, NL)
        reduced = jnp.where(live_mask[:, :, None], reduced, 0.0).astype(jnp.bfloat16)
        solved = jnp.einsum("prc,pcl->prl", inverse.astype(jnp.float32), reduced.astype(jnp.float32), precision=lax.Precision.HIGHEST)
        displaced = jnp.where(live_mask[:, :, None], solved, 0.0).astype(jnp.bfloat16).reshape(NN, 3 * NL)
        element = displaced[nodes_of.T].reshape(NE, 24, NL)
        strain = jnp.einsum("ije,ejl->eil", strain_map.astype(jnp.float32), element.astype(jnp.float32), precision=lax.Precision.HIGHEST)
        stress = jnp.einsum("ik,ekl->eil", elastic, strain, precision=lax.Precision.HIGHEST) * moduli[:, None, None]
        partial_value = jnp.zeros((NN, 6, NL), jnp.float32)
        for corner in range(8):
            partial_value = partial_value.at[nodes_of[corner]].add(stress)
        return displaced.reshape(NN, 3, NL), partial_value

    displacement, partials = lax.map(one_domain, (corner_values, coupling_all, force_all, inverse_all, panel_nodes, strain_all, modulus_all, connect_all))
    iface_rows = jax.vmap(pick_rows)(partials, interface).reshape(N_SUB, N_GRP, NIF, 6, NL)
    sub_lo = row_span(0, NIS)
    sub_hi = row_span(NIS, NIS)
    grp_lo = row_span(2 * NIS, NIG)
    grp_hi = row_span(2 * NIS + NIG, NIG)
    start_edge = 2 * NIS + 2 * NIG
    edge_ll = row_span(start_edge, NED)
    edge_lh = row_span(start_edge + NED, NED)
    edge_hl = row_span(start_edge + 2 * NED, NED)
    edge_hh = row_span(start_edge + 3 * NED, NED)
    pairings = [
        (np.concatenate([sub_hi, edge_hl, edge_hh]), np.concatenate([sub_lo, edge_ll, edge_lh]), 1, 0),
        (np.concatenate([sub_lo, edge_ll, edge_lh]), np.concatenate([sub_hi, edge_hl, edge_hh]), -1, 0),
        (np.concatenate([grp_hi, edge_lh, edge_hh]), np.concatenate([grp_lo, edge_ll, edge_hl]), 0, 1),
        (np.concatenate([grp_lo, edge_ll, edge_hl]), np.concatenate([grp_hi, edge_lh, edge_hh]), 0, -1),
        (edge_hh, edge_ll, 1, 1),
        (edge_hl, edge_lh, 1, -1),
        (edge_lh, edge_hl, -1, 1),
        (edge_ll, edge_hh, -1, -1),
    ]
    totals = iface_rows
    for sender, receiver, step_sub, step_grp in pairings:
        totals = totals.at[:, :, receiver].add(shifted(iface_rows[:, :, sender], step_sub, step_grp))
    totals = totals.reshape(SUBDOMAINS, NIF, 6, NL)
    summed = jax.vmap(put_rows)(partials, interface, totals)
    stress_out = (summed / nodal_volume.reshape(SUBDOMAINS, NN)[:, :, None, None]).astype(jnp.bfloat16)
    return displacement.reshape(NODES, 3, NL), stress_out.reshape(NODES, 6, NL)
```

```python
import functools

import jax
import jax.numpy as jnp
import numpy as np
from jax import lax
from jax.experimental import pallas as pl
from jax.experimental.pallas import tpu as pltpu
from jax.sharding import PartitionSpec as P

NIS = 64
NIG = 32
NED = 8

MESH = pl.DeviceIdType.MESH

POISSON = 0.3

SUB_LO = np.arange(0, NIS)
SUB_HI = np.arange(NIS, 2 * NIS)
GRP_LO = np.arange(2 * NIS, 2 * NIS + NIG)
GRP_HI = np.arange(2 * NIS + NIG, 2 * NIS + 2 * NIG)
_E0 = 2 * NIS + 2 * NIG
EDGE_LL = np.arange(_E0, _E0 + NED)
EDGE_LH = np.arange(_E0 + NED, _E0 + 2 * NED)
EDGE_HL = np.arange(_E0 + 2 * NED, _E0 + 3 * NED)
EDGE_HH = np.arange(_E0 + 3 * NED, _E0 + 4 * NED)

DIRECTIONS = (
    (1, 0, (SUB_HI, EDGE_HL, EDGE_HH), (SUB_LO, EDGE_LL, EDGE_LH)),
    (-1, 0, (SUB_LO, EDGE_LL, EDGE_LH), (SUB_HI, EDGE_HL, EDGE_HH)),
    (0, 1, (GRP_HI, EDGE_LH, EDGE_HH), (GRP_LO, EDGE_LL, EDGE_HL)),
    (0, -1, (GRP_LO, EDGE_LL, EDGE_HL), (GRP_HI, EDGE_LH, EDGE_HH)),
    (1, 1, (EDGE_HH,), (EDGE_LL,)),
    (1, -1, (EDGE_HL,), (EDGE_LH,)),
    (-1, 1, (EDGE_LH,), (EDGE_HL,)),
    (-1, -1, (EDGE_LL,), (EDGE_HH,)),
)
SEND_ENTRIES = np.concatenate([np.concatenate(d[2]) for d in DIRECTIONS])
RECV_ENTRIES = np.concatenate([np.concatenate(d[3]) for d in DIRECTIONS])
SLOT_ROWS = [sum(len(x) for x in d[2]) for d in DIRECTIONS]
SLOT_START = np.concatenate([[0], np.cumsum(SLOT_ROWS)])


def iso_matrix():
    lame_first = POISSON / ((1.0 + POISSON) * (1.0 - 2.0 * POISSON))
    shear_mod = 0.5 / (1.0 + POISSON)
    upper_block = jnp.full((3, 3), lame_first, jnp.float32) + jnp.eye(3, dtype=jnp.float32) * (
        2.0 * shear_mod
    )
    shear_block = jnp.eye(3, dtype=jnp.float32) * shear_mod
    zero_block = jnp.zeros((3, 3), jnp.float32)
    return jnp.concatenate(
        [
            jnp.concatenate([upper_block, zero_block], 1),
            jnp.concatenate([zero_block, shear_block], 1),
        ],
        0,
    )


def _above(i, n):
    return (i + n - 1) // n


def _below(i, n):
    return (2 * n - 2 - i) // n


def _step_ok(i, d, n):
    if d < 0:
        return _above(i, n)
    if d > 0:
        return _below(i, n)
    return 1


def coarse_kernel(n_sub, n_grp, block_ref, out_ref, buf, send_sem, recv_sem):
    s = lax.axis_index("sub")
    g = lax.axis_index("grp")
    barrier = pltpu.get_barrier_semaphore()

    def peers():
        for ds in (-1, 0, 1):
            for gt in range(n_grp):
                yield ds, gt

    def exists(ds, gt):
        conds = []
        if ds < 0:
            conds.append(s + ds >= 0)
        if ds > 0:
            conds.append(s + ds < n_sub)
        if ds == 0:
            conds.append(g != gt)
        cond = conds[0]
        for c in conds[1:]:
            cond = jnp.logical_and(cond, c)
        return cond

    for ds, gt in peers():
        def signal(ds=ds, gt=gt):
            pl.semaphore_signal(barrier, inc=1, device_id=(s + ds, gt), device_id_type=MESH)
        pl.when(exists(ds, gt))(signal)
    count = (n_grp - 1) + n_grp * (_above(s, n_sub) + _below(s, n_sub))
    pl.semaphore_wait(barrier, count)

    copies = []
    for ds, gt in peers():
        slot_there = (1 - ds) * n_grp + g
        copy = pltpu.make_async_remote_copy(
            src_ref=block_ref,
            dst_ref=buf.at[slot_there],
            send_sem=send_sem.at[(ds + 1) * n_grp + gt],
            recv_sem=recv_sem.at[slot_there],
            device_id=(s + ds, gt),
            device_id_type=MESH,
        )
        pl.when(exists(ds, gt))(copy.start)
        copies.append(copy)
    for (ds, gt), copy in zip(peers(), copies):
        pl.when(exists(ds, gt))(copy.wait_send)
    for dr in (-1, 0, 1):
        for gr in range(n_grp):
            slot_here = (dr + 1) * n_grp + gr
            recv = pltpu.make_async_remote_copy(
                src_ref=block_ref,
                dst_ref=buf.at[slot_here],
                send_sem=send_sem.at[slot_here],
                recv_sem=recv_sem.at[slot_here],
                device_id=(s + dr, gr),
                device_id_type=MESH,
            )
            cond = exists(dr, gr)

            def take(slot_here=slot_here, recv=recv):
                recv.wait_recv()
                out_ref[slot_here] = buf[slot_here]

            def clear(slot_here=slot_here):
                out_ref[slot_here] = jnp.zeros(out_ref.shape[1:], out_ref.dtype)

            pl.when(cond)(take)
            def own(slot_here=slot_here):
                out_ref[slot_here] = block_ref[...]

            if dr == 0:
                pl.when(g == gr)(own)
            else:
                pl.when(jnp.logical_not(cond))(clear)


def face_kernel(n_sub, n_grp, send_ref, out_ref, buf, send_sem, recv_sem):
    s = lax.axis_index("sub")
    g = lax.axis_index("grp")
    barrier = pltpu.get_barrier_semaphore()

    def exists(ds, dg):
        conds = []
        if ds < 0:
            conds.append(s + ds >= 0)
        if ds > 0:
            conds.append(s + ds < n_sub)
        if dg < 0:
            conds.append(g + dg >= 0)
        if dg > 0:
            conds.append(g + dg < n_grp)
        cond = conds[0]
        for c in conds[1:]:
            cond = jnp.logical_and(cond, c)
        return cond

    for ds, dg, _, _ in DIRECTIONS:
        def signal(ds=ds, dg=dg):
            pl.semaphore_signal(barrier, inc=1, device_id=(s + ds, g + dg), device_id_type=MESH)
        pl.when(exists(ds, dg))(signal)
    count = 0
    for ds, dg, _, _ in DIRECTIONS:
        count = count + _step_ok(s, ds, n_sub) * _step_ok(g, dg, n_grp)
    pl.semaphore_wait(barrier, count)

    copies = []
    for k, (ds, dg, _, _) in enumerate(DIRECTIONS):
        rows = pl.ds(int(SLOT_START[k]), int(SLOT_ROWS[k]))
        copy = pltpu.make_async_remote_copy(
            src_ref=send_ref.at[rows],
            dst_ref=buf.at[rows],
            send_sem=send_sem.at[k],
            recv_sem=recv_sem.at[k],
            device_id=(s + ds, g + dg),
            device_id_type=MESH,
        )
        pl.when(exists(ds, dg))(copy.start)
        copies.append(copy)
    for k, (ds, dg, _, _) in enumerate(DIRECTIONS):
        pl.when(exists(ds, dg))(copies[k].wait_send)
    for k, (ds, dg, _, _) in enumerate(DIRECTIONS):
        rows = pl.ds(int(SLOT_START[k]), int(SLOT_ROWS[k]))
        cond = exists(-ds, -dg)

        def take(rows=rows, k=k):
            copies[k].wait_recv()
            out_ref[rows, :] = buf[rows, :]

        def clear(rows=rows):
            out_ref[rows, :] = jnp.zeros((rows.size, out_ref.shape[1]), out_ref.dtype)

        pl.when(cond)(take)
        pl.when(jnp.logical_not(cond))(clear)


def fetch_coarse(block, n_sub, n_grp):
    rows, width = block.shape
    slots = 3 * n_grp
    out = pl.pallas_call(
        functools.partial(coarse_kernel, n_sub, n_grp),
        out_shape=jax.ShapeDtypeStruct((slots, rows, width), block.dtype),
        in_specs=[pl.BlockSpec(memory_space=pltpu.VMEM)],
        out_specs=pl.BlockSpec(memory_space=pltpu.VMEM),
        scratch_shapes=[
            pltpu.VMEM((slots, rows, width), block.dtype),
            pltpu.SemaphoreType.DMA((slots,)),
            pltpu.SemaphoreType.DMA((slots,)),
        ],
        compiler_params=pltpu.CompilerParams(collective_id=0, has_side_effects=True),
    )(block)
    return out.reshape(slots * rows, width)


def exchange_faces(send, n_sub, n_grp):
    return pl.pallas_call(
        functools.partial(face_kernel, n_sub, n_grp),
        out_shape=jax.ShapeDtypeStruct(send.shape, send.dtype),
        in_specs=[pl.BlockSpec(memory_space=pltpu.VMEM)],
        out_specs=pl.BlockSpec(memory_space=pltpu.VMEM),
        scratch_shapes=[
            pltpu.VMEM(send.shape, send.dtype),
            pltpu.SemaphoreType.DMA((len(DIRECTIONS),)),
            pltpu.SemaphoreType.DMA((len(DIRECTIONS),)),
        ],
        compiler_params=pltpu.CompilerParams(collective_id=1, has_side_effects=True),
    )(send)


def shards(
    n_sub,
    n_grp,
    coarse,
    corner_idx,
    coupling,
    force,
    panel_inv,
    panel_nodes,
    strain_disp,
    modulus,
    connect,
    interface,
    nodal_volume,
):
    nearby = fetch_coarse(coarse, n_sub, n_grp)
    block_rows = n_grp * coarse.shape[0]
    offset = (lax.axis_index("sub") - 1) * block_rows
    local_rows = corner_idx[0] - offset
    selector = (local_rows[:, None] == jnp.arange(3 * block_rows, dtype=jnp.int32)[None, :]).astype(
        jnp.float32
    )
    corner_vals = jnp.dot(selector, nearby, precision=lax.Precision.HIGHEST)
    node_count = force.shape[0]
    load_cases = force.shape[2]
    panels = panel_inv.shape[0]
    panel_rows = panel_inv.shape[1]
    correction = jnp.dot(coupling.astype(jnp.float32), corner_vals, precision=lax.Precision.HIGHEST)
    live_mask = jnp.arange(panel_rows)[None, :] < 3 * panel_nodes[0][:, None]
    reduced = (force.reshape(3 * node_count, load_cases).astype(jnp.float32) - correction).reshape(
        panels, panel_rows, load_cases
    )
    reduced = jnp.where(live_mask[:, :, None], reduced, 0.0).astype(jnp.bfloat16)
    solved = jnp.einsum("prc,pcl->prl", panel_inv, reduced, preferred_element_type=jnp.float32)
    displaced = (
        jnp.where(live_mask[:, :, None], solved, 0.0)
        .astype(jnp.bfloat16)
        .reshape(node_count, 3 * load_cases)
    )
    elem_count = connect.shape[1]
    element = displaced[connect.T].reshape(elem_count, 24, load_cases)
    strain = jnp.einsum("ije,ejl->eil", strain_disp, element, preferred_element_type=jnp.float32)
    stress = (
        jnp.einsum("ik,ekl->eil", iso_matrix(), strain, precision=lax.Precision.HIGHEST)
        * modulus[:, None, None]
    )
    node_range = jnp.arange(node_count, dtype=jnp.int32)
    incidence = jnp.sum(
        (connect[:, None, :] == node_range[None, :, None]).astype(jnp.float32), axis=0
    )
    partial_value = jnp.dot(
        incidence, stress.reshape(elem_count, 6 * load_cases), precision=lax.Precision.HIGHEST
    )
    node_ids = interface[0]
    send_ids = node_ids[SEND_ENTRIES]
    recv_ids = node_ids[RECV_ENTRIES]
    send_pick = (send_ids[:, None] == node_range[None, :]).astype(jnp.float32)
    recv_pick = (recv_ids[:, None] == node_range[None, :]).astype(jnp.float32)
    send = jnp.dot(send_pick, partial_value, precision=lax.Precision.HIGHEST)
    received = exchange_faces(send, n_sub, n_grp)
    summed = partial_value + jnp.dot(recv_pick.T, received, precision=lax.Precision.HIGHEST)
    stress_out = (summed.reshape(node_count, 6, load_cases) / nodal_volume[:, None, None]).astype(
        jnp.bfloat16
    )
    return (displaced.reshape(node_count, 3, load_cases), stress_out)


def solution(mesh):
    n_sub = mesh.shape["sub"]
    n_grp = mesh.shape["grp"]
    placed = (
        P(("sub", "grp"), None),
        P(("sub", "grp"), None),
        P(("sub", "grp"), None),
        P(("sub", "grp"), None, None),
        P(("sub", "grp"), None, None),
        P(("sub", "grp"), None),
        P(None, None, ("sub", "grp")),
        P(("sub", "grp")),
        P(None, ("sub", "grp")),
        P(("sub", "grp"), None),
        P(("sub", "grp")),
    )
    return jax.shard_map(
        functools.partial(shards, n_sub, n_grp),
        mesh=mesh,
        in_specs=placed,
        out_specs=(P(("sub", "grp"), None, None), P(("sub", "grp"), None, None)),
        check_vma=False,
    )
```

```python
import functools

import jax
import jax.numpy as jnp
import numpy as np
from jax import lax
from jax.experimental import pallas as pl
from jax.experimental.pallas import tpu as pltpu
from jax.sharding import PartitionSpec as P

NIS = 64
NIG = 32
NED = 8

MESH = pl.DeviceIdType.MESH

POISSON = 0.3

SUB_LO = np.arange(0, NIS)
SUB_HI = np.arange(NIS, 2 * NIS)
GRP_LO = np.arange(2 * NIS, 2 * NIS + NIG)
GRP_HI = np.arange(2 * NIS + NIG, 2 * NIS + 2 * NIG)
_E0 = 2 * NIS + 2 * NIG
EDGE_LL = np.arange(_E0, _E0 + NED)
EDGE_LH = np.arange(_E0 + NED, _E0 + 2 * NED)
EDGE_HL = np.arange(_E0 + 2 * NED, _E0 + 3 * NED)
EDGE_HH = np.arange(_E0 + 3 * NED, _E0 + 4 * NED)

DIRECTIONS = (
    (1, 0, (SUB_HI, EDGE_HL, EDGE_HH), (SUB_LO, EDGE_LL, EDGE_LH)),
    (-1, 0, (SUB_LO, EDGE_LL, EDGE_LH), (SUB_HI, EDGE_HL, EDGE_HH)),
    (0, 1, (GRP_HI, EDGE_LH, EDGE_HH), (GRP_LO, EDGE_LL, EDGE_HL)),
    (0, -1, (GRP_LO, EDGE_LL, EDGE_HL), (GRP_HI, EDGE_LH, EDGE_HH)),
    (1, 1, (EDGE_HH,), (EDGE_LL,)),
    (1, -1, (EDGE_HL,), (EDGE_LH,)),
    (-1, 1, (EDGE_LH,), (EDGE_HL,)),
    (-1, -1, (EDGE_LL,), (EDGE_HH,)),
)
SEND_ENTRIES = np.concatenate([np.concatenate(d[2]) for d in DIRECTIONS])
RECV_ENTRIES = np.concatenate([np.concatenate(d[3]) for d in DIRECTIONS])
SLOT_ROWS = [sum(len(x) for x in d[2]) for d in DIRECTIONS]
SLOT_START = np.concatenate([[0], np.cumsum(SLOT_ROWS)])


def _runs(entries):
    runs = []
    for i in entries:
        if runs and runs[-1][1] == i:
            runs[-1][1] = i + 1
        else:
            runs.append([i, i + 1])
    return runs


def iso_matrix():
    lame_first = POISSON / ((1.0 + POISSON) * (1.0 - 2.0 * POISSON))
    shear_mod = 0.5 / (1.0 + POISSON)
    upper_block = jnp.full((3, 3), lame_first, jnp.float32) + jnp.eye(3, dtype=jnp.float32) * (
        2.0 * shear_mod
    )
    shear_block = jnp.eye(3, dtype=jnp.float32) * shear_mod
    zero_block = jnp.zeros((3, 3), jnp.float32)
    return jnp.concatenate(
        [
            jnp.concatenate([upper_block, zero_block], 1),
            jnp.concatenate([zero_block, shear_block], 1),
        ],
        0,
    )


def _above(i, n):
    return (i + n - 1) // n


def _below(i, n):
    return (2 * n - 2 - i) // n


def _step_ok(i, d, n):
    if d < 0:
        return _above(i, n)
    if d > 0:
        return _below(i, n)
    return 1


def coarse_kernel(n_sub, n_grp, block_ref, out_ref, buf, send_sem, recv_sem):
    s = lax.axis_index("sub")
    g = lax.axis_index("grp")
    barrier = pltpu.get_barrier_semaphore()

    def peers():
        for ds in (-1, 0, 1):
            for gt in range(n_grp):
                yield ds, gt

    def exists(ds, gt):
        conds = []
        if ds < 0:
            conds.append(s + ds >= 0)
        if ds > 0:
            conds.append(s + ds < n_sub)
        if ds == 0:
            conds.append(g != gt)
        cond = conds[0]
        for c in conds[1:]:
            cond = jnp.logical_and(cond, c)
        return cond

    for ds, gt in peers():
        def signal(ds=ds, gt=gt):
            pl.semaphore_signal(barrier, inc=1, device_id=(s + ds, gt), device_id_type=MESH)
        pl.when(exists(ds, gt))(signal)
    count = (n_grp - 1) + n_grp * (_above(s, n_sub) + _below(s, n_sub))
    pl.semaphore_wait(barrier, count)

    copies = []
    for ds, gt in peers():
        slot_there = (1 - ds) * n_grp + g
        copy = pltpu.make_async_remote_copy(
            src_ref=block_ref,
            dst_ref=buf.at[slot_there],
            send_sem=send_sem.at[(ds + 1) * n_grp + gt],
            recv_sem=recv_sem.at[slot_there],
            device_id=(s + ds, gt),
            device_id_type=MESH,
        )
        pl.when(exists(ds, gt))(copy.start)
        copies.append(copy)
    for (ds, gt), copy in zip(peers(), copies):
        pl.when(exists(ds, gt))(copy.wait_send)
    for dr in (-1, 0, 1):
        for gr in range(n_grp):
            slot_here = (dr + 1) * n_grp + gr
            recv = pltpu.make_async_remote_copy(
                src_ref=block_ref,
                dst_ref=buf.at[slot_here],
                send_sem=send_sem.at[slot_here],
                recv_sem=recv_sem.at[slot_here],
                device_id=(s + dr, gr),
                device_id_type=MESH,
            )
            cond = exists(dr, gr)

            def take(slot_here=slot_here, recv=recv):
                recv.wait_recv()
                out_ref[slot_here] = buf[slot_here]

            def clear(slot_here=slot_here):
                out_ref[slot_here] = jnp.zeros(out_ref.shape[1:], out_ref.dtype)

            pl.when(cond)(take)
            def own(slot_here=slot_here):
                out_ref[slot_here] = block_ref[...]

            if dr == 0:
                pl.when(g == gr)(own)
            else:
                pl.when(jnp.logical_not(cond))(clear)


def face_kernel(n_sub, n_grp, send_ref, out_ref, buf, send_sem, recv_sem):
    s = lax.axis_index("sub")
    g = lax.axis_index("grp")
    barrier = pltpu.get_barrier_semaphore()

    def exists(ds, dg):
        conds = []
        if ds < 0:
            conds.append(s + ds >= 0)
        if ds > 0:
            conds.append(s + ds < n_sub)
        if dg < 0:
            conds.append(g + dg >= 0)
        if dg > 0:
            conds.append(g + dg < n_grp)
        cond = conds[0]
        for c in conds[1:]:
            cond = jnp.logical_and(cond, c)
        return cond

    for ds, dg, _, _ in DIRECTIONS:
        def signal(ds=ds, dg=dg):
            pl.semaphore_signal(barrier, inc=1, device_id=(s + ds, g + dg), device_id_type=MESH)
        pl.when(exists(ds, dg))(signal)
    count = 0
    for ds, dg, _, _ in DIRECTIONS:
        count = count + _step_ok(s, ds, n_sub) * _step_ok(g, dg, n_grp)
    pl.semaphore_wait(barrier, count)

    copies = []
    for k, (ds, dg, _, _) in enumerate(DIRECTIONS):
        rows = pl.ds(int(SLOT_START[k]), int(SLOT_ROWS[k]))
        copy = pltpu.make_async_remote_copy(
            src_ref=send_ref.at[:, rows],
            dst_ref=buf.at[:, rows],
            send_sem=send_sem.at[k],
            recv_sem=recv_sem.at[k],
            device_id=(s + ds, g + dg),
            device_id_type=MESH,
        )
        pl.when(exists(ds, dg))(copy.start)
        copies.append(copy)
    for k, (ds, dg, _, _) in enumerate(DIRECTIONS):
        pl.when(exists(ds, dg))(copies[k].wait_send)
    for k, (ds, dg, _, _) in enumerate(DIRECTIONS):
        rows = pl.ds(int(SLOT_START[k]), int(SLOT_ROWS[k]))
        cond = exists(-ds, -dg)

        def take(rows=rows, k=k):
            copies[k].wait_recv()
            out_ref[:, rows, :] = buf[:, rows, :]

        def clear(rows=rows):
            out_ref[:, rows, :] = jnp.zeros(
                (out_ref.shape[0], rows.size, out_ref.shape[2]), out_ref.dtype
            )

        pl.when(cond)(take)
        pl.when(jnp.logical_not(cond))(clear)


def fetch_coarse(block, n_sub, n_grp):
    rows, width = block.shape
    slots = 3 * n_grp
    out = pl.pallas_call(
        functools.partial(coarse_kernel, n_sub, n_grp),
        out_shape=jax.ShapeDtypeStruct((slots, rows, width), block.dtype),
        in_specs=[pl.BlockSpec(memory_space=pltpu.VMEM)],
        out_specs=pl.BlockSpec(memory_space=pltpu.VMEM),
        scratch_shapes=[
            pltpu.VMEM((slots, rows, width), block.dtype),
            pltpu.SemaphoreType.DMA((slots,)),
            pltpu.SemaphoreType.DMA((slots,)),
        ],
        compiler_params=pltpu.CompilerParams(collective_id=0, has_side_effects=True),
    )(block)
    return out.reshape(slots * rows, width)


def exchange_faces(send, n_sub, n_grp):
    return pl.pallas_call(
        functools.partial(face_kernel, n_sub, n_grp),
        out_shape=jax.ShapeDtypeStruct(send.shape, send.dtype),
        in_specs=[pl.BlockSpec(memory_space=pltpu.VMEM)],
        out_specs=pl.BlockSpec(memory_space=pltpu.VMEM),
        scratch_shapes=[
            pltpu.VMEM(send.shape, send.dtype),
            pltpu.SemaphoreType.DMA((len(DIRECTIONS),)),
            pltpu.SemaphoreType.DMA((len(DIRECTIONS),)),
        ],
        compiler_params=pltpu.CompilerParams(collective_id=1, has_side_effects=True),
    )(send)


def shards(
    n_sub,
    n_grp,
    coarse,
    corner_idx,
    coupling,
    force,
    panel_inv,
    panel_nodes,
    strain_disp,
    modulus,
    connect,
    interface,
    nodal_volume,
):
    nearby = fetch_coarse(coarse, n_sub, n_grp)
    block_rows = n_grp * coarse.shape[0]
    offset = (lax.axis_index("sub") - 1) * block_rows
    local_rows = corner_idx[0] - offset
    selector = (local_rows[:, None] == jnp.arange(3 * block_rows, dtype=jnp.int32)[None, :]).astype(
        jnp.float32
    )
    corner_vals = jnp.dot(selector, nearby, precision=lax.Precision.HIGHEST)
    node_count = force.shape[0]
    load_cases = force.shape[2]
    panels = panel_inv.shape[0]
    panel_rows = panel_inv.shape[1]
    correction = jnp.dot(coupling.astype(jnp.float32), corner_vals, precision=lax.Precision.HIGHEST)
    live_mask = jnp.arange(panel_rows)[None, :] < 3 * panel_nodes[0][:, None]
    reduced = (force.reshape(3 * node_count, load_cases).astype(jnp.float32) - correction).reshape(
        panels, panel_rows, load_cases
    )
    reduced = jnp.where(live_mask[:, :, None], reduced, 0.0).astype(jnp.bfloat16)
    solved = jnp.einsum("prc,pcl->prl", panel_inv, reduced, preferred_element_type=jnp.float32)
    displaced = (
        jnp.where(live_mask[:, :, None], solved, 0.0)
        .astype(jnp.bfloat16)
        .reshape(node_count, 3 * load_cases)
    )
    elem_count = connect.shape[1]
    node_range = jnp.arange(node_count, dtype=jnp.int32)
    corner_of = (connect.T.reshape(-1)[:, None] == node_range[None, :]).astype(jnp.bfloat16)
    element = jnp.dot(corner_of, displaced, preferred_element_type=jnp.float32)
    element = element.astype(jnp.bfloat16).reshape(elem_count, 24, load_cases)
    strain = jnp.einsum("ije,ejl->eil", strain_disp, element, preferred_element_type=jnp.float32)
    stress = (
        jnp.einsum("ik,ekl->iel", iso_matrix(), strain, precision=lax.Precision.HIGHEST)
        * modulus[None, :, None]
    )
    incidence = jnp.sum(
        (connect[:, None, :] == node_range[None, :, None]).astype(jnp.float32), axis=0
    )
    partial_value = jnp.einsum(
        "ne,cel->cnl", incidence, stress, precision=lax.Precision.HIGHEST
    )
    node_ids = interface[0]
    send_ids = jnp.concatenate([node_ids[int(a):int(b)] for a, b in _runs(SEND_ENTRIES)])
    recv_ids = jnp.concatenate([node_ids[int(a):int(b)] for a, b in _runs(RECV_ENTRIES)])
    send_pick = (send_ids[:, None] == node_range[None, :]).astype(jnp.float32)
    recv_pick = (recv_ids[:, None] == node_range[None, :]).astype(jnp.float32)
    send_count = jnp.dot(send_pick, incidence)
    send = jnp.einsum("re,cel->crl", send_count, stress, precision=lax.Precision.HIGHEST)
    received = exchange_faces(send, n_sub, n_grp)
    summed = partial_value + jnp.einsum(
        "rn,crl->cnl", recv_pick, received, precision=lax.Precision.HIGHEST
    )
    stress_out = (summed / nodal_volume[None, :, None]).astype(jnp.bfloat16).transpose(1, 0, 2)
    return (displaced.reshape(node_count, 3, load_cases), stress_out)


def solution(mesh):
    n_sub = mesh.shape["sub"]
    n_grp = mesh.shape["grp"]
    placed = (
        P(("sub", "grp"), None),
        P(("sub", "grp"), None),
        P(("sub", "grp"), None),
        P(("sub", "grp"), None, None),
        P(("sub", "grp"), None, None),
        P(("sub", "grp"), None),
        P(None, None, ("sub", "grp")),
        P(("sub", "grp")),
        P(None, ("sub", "grp")),
        P(("sub", "grp"), None),
        P(("sub", "grp")),
    )
    return jax.shard_map(
        functools.partial(shards, n_sub, n_grp),
        mesh=mesh,
        in_specs=placed,
        out_specs=(P(("sub", "grp"), None, None), P(("sub", "grp"), None, None)),
        check_vma=False,
    )
```

```python
import functools

import jax
import jax.numpy as jnp
import numpy as np
from jax import lax
from jax.experimental import pallas as pl
from jax.experimental.pallas import tpu as pltpu
from jax.sharding import PartitionSpec as P

NIS = 64
NIG = 32
NED = 8

MESH = pl.DeviceIdType.MESH

POISSON = 0.3

SUB_LO = np.arange(0, NIS)
SUB_HI = np.arange(NIS, 2 * NIS)
GRP_LO = np.arange(2 * NIS, 2 * NIS + NIG)
GRP_HI = np.arange(2 * NIS + NIG, 2 * NIS + 2 * NIG)
_E0 = 2 * NIS + 2 * NIG
EDGE_LL = np.arange(_E0, _E0 + NED)
EDGE_LH = np.arange(_E0 + NED, _E0 + 2 * NED)
EDGE_HL = np.arange(_E0 + 2 * NED, _E0 + 3 * NED)
EDGE_HH = np.arange(_E0 + 3 * NED, _E0 + 4 * NED)

DIRECTIONS = (
    (1, 0, (SUB_HI, EDGE_HL, EDGE_HH), (SUB_LO, EDGE_LL, EDGE_LH)),
    (-1, 0, (SUB_LO, EDGE_LL, EDGE_LH), (SUB_HI, EDGE_HL, EDGE_HH)),
    (0, 1, (GRP_HI, EDGE_LH, EDGE_HH), (GRP_LO, EDGE_LL, EDGE_HL)),
    (0, -1, (GRP_LO, EDGE_LL, EDGE_HL), (GRP_HI, EDGE_LH, EDGE_HH)),
    (1, 1, (EDGE_HH,), (EDGE_LL,)),
    (1, -1, (EDGE_HL,), (EDGE_LH,)),
    (-1, 1, (EDGE_LH,), (EDGE_HL,)),
    (-1, -1, (EDGE_LL,), (EDGE_HH,)),
)
SLOT_ROWS = [sum(len(x) for x in d[2]) for d in DIRECTIONS]
SLOT_START = np.concatenate([[0], np.cumsum(SLOT_ROWS)])


def _runs(entries):
    runs = []
    for i in entries:
        if runs and runs[-1][1] == i:
            runs[-1][1] = i + 1
        else:
            runs.append([i, i + 1])
    return [(int(a), int(b)) for a, b in runs]


def _pieces(k, which):
    out = []
    row = int(SLOT_START[k])
    for a, b in _runs(np.concatenate(DIRECTIONS[k][which])):
        out.append((a, b, row))
        row += b - a
    return out


SEND_PIECES = [(k, a, b, row) for k in range(len(DIRECTIONS)) for a, b, row in _pieces(k, 2)]
RECV_PIECES = [_pieces(k, 3) for k in range(len(DIRECTIONS))]


def iso_matrix():
    lame_first = POISSON / ((1.0 + POISSON) * (1.0 - 2.0 * POISSON))
    shear_mod = 0.5 / (1.0 + POISSON)
    upper_block = jnp.full((3, 3), lame_first, jnp.float32) + jnp.eye(3, dtype=jnp.float32) * (
        2.0 * shear_mod
    )
    shear_block = jnp.eye(3, dtype=jnp.float32) * shear_mod
    zero_block = jnp.zeros((3, 3), jnp.float32)
    return jnp.concatenate(
        [
            jnp.concatenate([upper_block, zero_block], 1),
            jnp.concatenate([zero_block, shear_block], 1),
        ],
        0,
    )


def _above(i, n):
    return (i + n - 1) // n


def _below(i, n):
    return (2 * n - 2 - i) // n


def _step_ok(i, d, n):
    if d < 0:
        return _above(i, n)
    if d > 0:
        return _below(i, n)
    return 1


def coarse_kernel(n_sub, n_grp, block_ref, out_ref, buf, send_sem, recv_sem):
    s = lax.axis_index("sub")
    g = lax.axis_index("grp")
    barrier = pltpu.get_barrier_semaphore()

    def peers():
        for ds in (-1, 0, 1):
            for gt in range(n_grp):
                yield ds, gt

    def exists(ds, gt):
        conds = []
        if ds < 0:
            conds.append(s + ds >= 0)
        if ds > 0:
            conds.append(s + ds < n_sub)
        if ds == 0:
            conds.append(g != gt)
        cond = conds[0]
        for c in conds[1:]:
            cond = jnp.logical_and(cond, c)
        return cond

    for ds, gt in peers():
        def signal(ds=ds, gt=gt):
            pl.semaphore_signal(barrier, inc=1, device_id=(s + ds, gt), device_id_type=MESH)
        pl.when(exists(ds, gt))(signal)
    count = (n_grp - 1) + n_grp * (_above(s, n_sub) + _below(s, n_sub))
    pl.semaphore_wait(barrier, count)

    copies = []
    for ds, gt in peers():
        slot_there = (1 - ds) * n_grp + g
        copy = pltpu.make_async_remote_copy(
            src_ref=block_ref,
            dst_ref=buf.at[slot_there],
            send_sem=send_sem.at[(ds + 1) * n_grp + gt],
            recv_sem=recv_sem.at[slot_there],
            device_id=(s + ds, gt),
            device_id_type=MESH,
        )
        pl.when(exists(ds, gt))(copy.start)
        copies.append(copy)
    for (ds, gt), copy in zip(peers(), copies):
        pl.when(exists(ds, gt))(copy.wait_send)
    for dr in (-1, 0, 1):
        for gr in range(n_grp):
            slot_here = (dr + 1) * n_grp + gr
            recv = pltpu.make_async_remote_copy(
                src_ref=block_ref,
                dst_ref=buf.at[slot_here],
                send_sem=send_sem.at[slot_here],
                recv_sem=recv_sem.at[slot_here],
                device_id=(s + dr, gr),
                device_id_type=MESH,
            )
            cond = exists(dr, gr)

            def take(slot_here=slot_here, recv=recv):
                recv.wait_recv()
                out_ref[slot_here] = buf[slot_here]

            def clear(slot_here=slot_here):
                out_ref[slot_here] = jnp.zeros(out_ref.shape[1:], out_ref.dtype)

            pl.when(cond)(take)
            def own(slot_here=slot_here):
                out_ref[slot_here] = block_ref[...]

            if dr == 0:
                pl.when(g == gr)(own)
            else:
                pl.when(jnp.logical_not(cond))(clear)


def face_kernel(n_sub, n_grp, send_ref, out_ref, buf, send_sem, recv_sem):
    s = lax.axis_index("sub")
    g = lax.axis_index("grp")
    barrier = pltpu.get_barrier_semaphore()

    def exists(ds, dg):
        conds = []
        if ds < 0:
            conds.append(s + ds >= 0)
        if ds > 0:
            conds.append(s + ds < n_sub)
        if dg < 0:
            conds.append(g + dg >= 0)
        if dg > 0:
            conds.append(g + dg < n_grp)
        cond = conds[0]
        for c in conds[1:]:
            cond = jnp.logical_and(cond, c)
        return cond

    for ds, dg, _, _ in DIRECTIONS:
        def signal(ds=ds, dg=dg):
            pl.semaphore_signal(barrier, inc=1, device_id=(s + ds, g + dg), device_id_type=MESH)
        pl.when(exists(ds, dg))(signal)
    count = 0
    for ds, dg, _, _ in DIRECTIONS:
        count = count + _step_ok(s, ds, n_sub) * _step_ok(g, dg, n_grp)
    pl.semaphore_wait(barrier, count)

    copies = []
    for j, (k, lo, hi, row) in enumerate(SEND_PIECES):
        ds, dg = DIRECTIONS[k][:2]
        copy = pltpu.make_async_remote_copy(
            src_ref=send_ref.at[:, pl.ds(lo, hi - lo)],
            dst_ref=buf.at[:, pl.ds(row, hi - lo)],
            send_sem=send_sem.at[j],
            recv_sem=recv_sem.at[j],
            device_id=(s + ds, g + dg),
            device_id_type=MESH,
        )
        pl.when(exists(ds, dg))(copy.start)
        copies.append(copy)
    out_ref[...] = jnp.zeros(out_ref.shape, out_ref.dtype)
    for j, (k, lo, hi, row) in enumerate(SEND_PIECES):
        ds, dg = DIRECTIONS[k][:2]
        pl.when(exists(ds, dg))(copies[j].wait_send)
    for k, (ds, dg, _, _) in enumerate(DIRECTIONS):
        mine = [j for j, piece in enumerate(SEND_PIECES) if piece[0] == k]

        def take(k=k, mine=mine):
            for j in mine:
                copies[j].wait_recv()
            for lo, hi, row in RECV_PIECES[k]:
                out_ref[:, lo:hi, :] += buf[:, row:row + hi - lo, :]

        pl.when(exists(-ds, -dg))(take)


def fetch_coarse(block, n_sub, n_grp):
    rows, width = block.shape
    slots = 3 * n_grp
    out = pl.pallas_call(
        functools.partial(coarse_kernel, n_sub, n_grp),
        out_shape=jax.ShapeDtypeStruct((slots, rows, width), block.dtype),
        in_specs=[pl.BlockSpec(memory_space=pltpu.VMEM)],
        out_specs=pl.BlockSpec(memory_space=pltpu.VMEM),
        scratch_shapes=[
            pltpu.VMEM((slots, rows, width), block.dtype),
            pltpu.SemaphoreType.DMA((slots,)),
            pltpu.SemaphoreType.DMA((slots,)),
        ],
        compiler_params=pltpu.CompilerParams(collective_id=0, has_side_effects=True),
    )(block)
    return out.reshape(slots * rows, width)


def exchange_faces(send, n_sub, n_grp):
    return pl.pallas_call(
        functools.partial(face_kernel, n_sub, n_grp),
        out_shape=jax.ShapeDtypeStruct(send.shape, send.dtype),
        in_specs=[pl.BlockSpec(memory_space=pltpu.VMEM)],
        out_specs=pl.BlockSpec(memory_space=pltpu.VMEM),
        scratch_shapes=[
            pltpu.VMEM((send.shape[0], int(SLOT_START[-1]), send.shape[2]), send.dtype),
            pltpu.SemaphoreType.DMA((len(SEND_PIECES),)),
            pltpu.SemaphoreType.DMA((len(SEND_PIECES),)),
        ],
        compiler_params=pltpu.CompilerParams(collective_id=1, has_side_effects=True),
    )(send)


def shards(
    n_sub,
    n_grp,
    coarse,
    corner_idx,
    coupling,
    force,
    panel_inv,
    panel_nodes,
    strain_disp,
    modulus,
    connect,
    interface,
    nodal_volume,
):
    nearby = fetch_coarse(coarse, n_sub, n_grp)
    block_rows = n_grp * coarse.shape[0]
    offset = (lax.axis_index("sub") - 1) * block_rows
    local_rows = corner_idx[0] - offset
    selector = (local_rows[:, None] == jnp.arange(3 * block_rows, dtype=jnp.int32)[None, :]).astype(
        jnp.float32
    )
    corner_vals = jnp.dot(selector, nearby, precision=lax.Precision.HIGHEST)
    node_count = force.shape[0]
    load_cases = force.shape[2]
    panels = panel_inv.shape[0]
    panel_rows = panel_inv.shape[1]
    correction = jnp.dot(coupling.astype(jnp.float32), corner_vals, precision=lax.Precision.HIGHEST)
    live_mask = jnp.arange(panel_rows)[None, :] < 3 * panel_nodes[0][:, None]
    reduced = (force.reshape(3 * node_count, load_cases).astype(jnp.float32) - correction).reshape(
        panels, panel_rows, load_cases
    )
    reduced = jnp.where(live_mask[:, :, None], reduced, 0.0).astype(jnp.bfloat16)
    solved = jnp.einsum("prc,pcl->prl", panel_inv, reduced, preferred_element_type=jnp.float32)
    displaced = (
        jnp.where(live_mask[:, :, None], solved, 0.0)
        .astype(jnp.bfloat16)
        .reshape(node_count, 3 * load_cases)
    )
    elem_count = connect.shape[1]
    node_range = jnp.arange(node_count, dtype=jnp.int32)
    corner_of = (connect.T.reshape(-1)[:, None] == node_range[None, :]).astype(jnp.bfloat16)
    element = jnp.dot(corner_of, displaced, preferred_element_type=jnp.float32)
    element = element.astype(jnp.bfloat16).reshape(elem_count, 24, load_cases)
    strain = jnp.einsum("ije,ejl->eil", strain_disp, element, preferred_element_type=jnp.float32)
    stress = (
        jnp.einsum("ik,ekl->iel", iso_matrix(), strain, precision=lax.Precision.HIGHEST)
        * modulus[None, :, None]
    )
    incidence = jnp.sum(
        (connect[:, None, :] == node_range[None, :, None]).astype(jnp.float32), axis=0
    )
    partial_value = jnp.einsum(
        "ne,cel->cnl", incidence, stress, precision=lax.Precision.HIGHEST
    )
    picker = (interface[0][:, None] == node_range[None, :]).astype(jnp.float32)
    iface_count = jnp.dot(picker, incidence)
    send = jnp.einsum("re,cel->crl", iface_count, stress, precision=lax.Precision.HIGHEST)
    added = exchange_faces(send, n_sub, n_grp)
    summed = partial_value + jnp.einsum(
        "rn,crl->cnl", picker, added, precision=lax.Precision.HIGHEST
    )
    stress_out = (summed / nodal_volume[None, :, None]).astype(jnp.bfloat16).transpose(1, 0, 2)
    return (displaced.reshape(node_count, 3, load_cases), stress_out)


def solution(mesh):
    n_sub = mesh.shape["sub"]
    n_grp = mesh.shape["grp"]
    placed = (
        P(("sub", "grp"), None),
        P(("sub", "grp"), None),
        P(("sub", "grp"), None),
        P(("sub", "grp"), None, None),
        P(("sub", "grp"), None, None),
        P(("sub", "grp"), None),
        P(None, None, ("sub", "grp")),
        P(("sub", "grp")),
        P(None, ("sub", "grp")),
        P(("sub", "grp"), None),
        P(("sub", "grp")),
    )
    return jax.shard_map(
        functools.partial(shards, n_sub, n_grp),
        mesh=mesh,
        in_specs=placed,
        out_specs=(P(("sub", "grp"), None, None), P(("sub", "grp"), None, None)),
        check_vma=False,
    )
```

```python
import functools

import jax
import jax.numpy as jnp
import numpy as np
from jax import lax
from jax.experimental import pallas as pl
from jax.experimental.pallas import tpu as pltpu
from jax.sharding import PartitionSpec as P

NIS = 64
NIG = 32
NED = 8

MESH = pl.DeviceIdType.MESH

POISSON = 0.3

SUB_LO = np.arange(0, NIS)
SUB_HI = np.arange(NIS, 2 * NIS)
GRP_LO = np.arange(2 * NIS, 2 * NIS + NIG)
GRP_HI = np.arange(2 * NIS + NIG, 2 * NIS + 2 * NIG)
_E0 = 2 * NIS + 2 * NIG
EDGE_LL = np.arange(_E0, _E0 + NED)
EDGE_LH = np.arange(_E0 + NED, _E0 + 2 * NED)
EDGE_HL = np.arange(_E0 + 2 * NED, _E0 + 3 * NED)
EDGE_HH = np.arange(_E0 + 3 * NED, _E0 + 4 * NED)

DIRECTIONS = (
    (1, 0, (SUB_HI, EDGE_HL, EDGE_HH), (SUB_LO, EDGE_LL, EDGE_LH)),
    (-1, 0, (SUB_LO, EDGE_LL, EDGE_LH), (SUB_HI, EDGE_HL, EDGE_HH)),
    (0, 1, (GRP_HI, EDGE_LH, EDGE_HH), (GRP_LO, EDGE_LL, EDGE_HL)),
    (0, -1, (GRP_LO, EDGE_LL, EDGE_HL), (GRP_HI, EDGE_LH, EDGE_HH)),
    (1, 1, (EDGE_HH,), (EDGE_LL,)),
    (1, -1, (EDGE_HL,), (EDGE_LH,)),
    (-1, 1, (EDGE_LH,), (EDGE_HL,)),
    (-1, -1, (EDGE_LL,), (EDGE_HH,)),
)
SLOT_ROWS = [sum(len(x) for x in d[2]) for d in DIRECTIONS]
SLOT_START = np.concatenate([[0], np.cumsum(SLOT_ROWS)])


def _runs(entries):
    runs = []
    for i in entries:
        if runs and runs[-1][1] == i:
            runs[-1][1] = i + 1
        else:
            runs.append([i, i + 1])
    return [(int(a), int(b)) for a, b in runs]


def _pieces(k, which):
    out = []
    row = int(SLOT_START[k])
    for a, b in _runs(np.concatenate(DIRECTIONS[k][which])):
        out.append((a, b, row))
        row += b - a
    return out


SEND_PIECES = [(k, a, b, row) for k in range(len(DIRECTIONS)) for a, b, row in _pieces(k, 2)]
RECV_PIECES = [_pieces(k, 3) for k in range(len(DIRECTIONS))]


def iso_matrix():
    lame_first = POISSON / ((1.0 + POISSON) * (1.0 - 2.0 * POISSON))
    shear_mod = 0.5 / (1.0 + POISSON)
    elastic = np.zeros((6, 6), np.float32)
    elastic[:3, :3] = lame_first
    elastic[:3, :3] += np.eye(3, dtype=np.float32) * np.float32(2.0 * shear_mod)
    elastic[3:, 3:] = np.eye(3, dtype=np.float32) * np.float32(shear_mod)
    return elastic


def _above(i, n):
    return (i + n - 1) // n


def _below(i, n):
    return (2 * n - 2 - i) // n


def _step_ok(i, d, n):
    if d < 0:
        return _above(i, n)
    if d > 0:
        return _below(i, n)
    return 1


def coarse_kernel(n_sub, n_grp, block_ref, out_ref, buf, send_sem, recv_sem):
    s = lax.axis_index("sub")
    g = lax.axis_index("grp")
    barrier = pltpu.get_barrier_semaphore()

    def peers():
        for ds in (-1, 0, 1):
            for gt in range(n_grp):
                yield ds, gt

    def exists(ds, gt):
        conds = []
        if ds < 0:
            conds.append(s + ds >= 0)
        if ds > 0:
            conds.append(s + ds < n_sub)
        if ds == 0:
            conds.append(g != gt)
        cond = conds[0]
        for c in conds[1:]:
            cond = jnp.logical_and(cond, c)
        return cond

    for ds, gt in peers():
        def signal(ds=ds, gt=gt):
            pl.semaphore_signal(barrier, inc=1, device_id=(s + ds, gt), device_id_type=MESH)
        pl.when(exists(ds, gt))(signal)
    count = (n_grp - 1) + n_grp * (_above(s, n_sub) + _below(s, n_sub))
    pl.semaphore_wait(barrier, count)

    copies = []
    for ds, gt in peers():
        slot_there = (1 - ds) * n_grp + g
        copy = pltpu.make_async_remote_copy(
            src_ref=block_ref,
            dst_ref=buf.at[slot_there],
            send_sem=send_sem.at[(ds + 1) * n_grp + gt],
            recv_sem=recv_sem.at[slot_there],
            device_id=(s + ds, gt),
            device_id_type=MESH,
        )
        pl.when(exists(ds, gt))(copy.start)
        copies.append(copy)
    for (ds, gt), copy in zip(peers(), copies):
        pl.when(exists(ds, gt))(copy.wait_send)
    for dr in (-1, 0, 1):
        for gr in range(n_grp):
            slot_here = (dr + 1) * n_grp + gr
            recv = pltpu.make_async_remote_copy(
                src_ref=block_ref,
                dst_ref=buf.at[slot_here],
                send_sem=send_sem.at[slot_here],
                recv_sem=recv_sem.at[slot_here],
                device_id=(s + dr, gr),
                device_id_type=MESH,
            )
            cond = exists(dr, gr)

            def take(slot_here=slot_here, recv=recv):
                recv.wait_recv()
                out_ref[slot_here] = buf[slot_here]

            def clear(slot_here=slot_here):
                out_ref[slot_here] = jnp.zeros(out_ref.shape[1:], out_ref.dtype)

            pl.when(cond)(take)
            def own(slot_here=slot_here):
                out_ref[slot_here] = block_ref[...]

            if dr == 0:
                pl.when(g == gr)(own)
            else:
                pl.when(jnp.logical_not(cond))(clear)


def face_kernel(n_sub, n_grp, send_ref, out_ref, buf, send_sem, recv_sem):
    s = lax.axis_index("sub")
    g = lax.axis_index("grp")
    barrier = pltpu.get_barrier_semaphore()

    def exists(ds, dg):
        conds = []
        if ds < 0:
            conds.append(s + ds >= 0)
        if ds > 0:
            conds.append(s + ds < n_sub)
        if dg < 0:
            conds.append(g + dg >= 0)
        if dg > 0:
            conds.append(g + dg < n_grp)
        cond = conds[0]
        for c in conds[1:]:
            cond = jnp.logical_and(cond, c)
        return cond

    for ds, dg, _, _ in DIRECTIONS:
        def signal(ds=ds, dg=dg):
            pl.semaphore_signal(barrier, inc=1, device_id=(s + ds, g + dg), device_id_type=MESH)
        pl.when(exists(ds, dg))(signal)
    count = 0
    for ds, dg, _, _ in DIRECTIONS:
        count = count + _step_ok(s, ds, n_sub) * _step_ok(g, dg, n_grp)
    pl.semaphore_wait(barrier, count)

    copies = []
    for j, (k, lo, hi, row) in enumerate(SEND_PIECES):
        ds, dg = DIRECTIONS[k][:2]
        copy = pltpu.make_async_remote_copy(
            src_ref=send_ref.at[:, pl.ds(lo, hi - lo)],
            dst_ref=buf.at[:, pl.ds(row, hi - lo)],
            send_sem=send_sem.at[j],
            recv_sem=recv_sem.at[j],
            device_id=(s + ds, g + dg),
            device_id_type=MESH,
        )
        pl.when(exists(ds, dg))(copy.start)
        copies.append(copy)
    out_ref[...] = jnp.zeros(out_ref.shape, out_ref.dtype)
    for j, (k, lo, hi, row) in enumerate(SEND_PIECES):
        ds, dg = DIRECTIONS[k][:2]
        pl.when(exists(ds, dg))(copies[j].wait_send)
    for k, (ds, dg, _, _) in enumerate(DIRECTIONS):
        mine = [j for j, piece in enumerate(SEND_PIECES) if piece[0] == k]

        def take(k=k, mine=mine):
            for j in mine:
                copies[j].wait_recv()
            for lo, hi, row in RECV_PIECES[k]:
                out_ref[:, lo:hi, :] += buf[:, row:row + hi - lo, :]

        pl.when(exists(-ds, -dg))(take)


def fetch_coarse(block, n_sub, n_grp):
    rows, width = block.shape
    slots = 3 * n_grp
    out = pl.pallas_call(
        functools.partial(coarse_kernel, n_sub, n_grp),
        out_shape=jax.ShapeDtypeStruct((slots, rows, width), block.dtype),
        in_specs=[pl.BlockSpec(memory_space=pltpu.VMEM)],
        out_specs=pl.BlockSpec(memory_space=pltpu.VMEM),
        scratch_shapes=[
            pltpu.VMEM((slots, rows, width), block.dtype),
            pltpu.SemaphoreType.DMA((slots,)),
            pltpu.SemaphoreType.DMA((slots,)),
        ],
        compiler_params=pltpu.CompilerParams(collective_id=0, has_side_effects=True),
    )(block)
    return out.reshape(slots * rows, width)


def exchange_faces(send, n_sub, n_grp):
    return pl.pallas_call(
        functools.partial(face_kernel, n_sub, n_grp),
        out_shape=jax.ShapeDtypeStruct(send.shape, send.dtype),
        in_specs=[pl.BlockSpec(memory_space=pltpu.VMEM)],
        out_specs=pl.BlockSpec(memory_space=pltpu.VMEM),
        scratch_shapes=[
            pltpu.VMEM((send.shape[0], int(SLOT_START[-1]), send.shape[2]), send.dtype),
            pltpu.SemaphoreType.DMA((len(SEND_PIECES),)),
            pltpu.SemaphoreType.DMA((len(SEND_PIECES),)),
        ],
        compiler_params=pltpu.CompilerParams(collective_id=1, has_side_effects=True),
    )(send)


def shards(
    n_sub,
    n_grp,
    coarse,
    corner_idx,
    coupling,
    force,
    panel_inv,
    panel_nodes,
    strain_disp,
    modulus,
    connect,
    interface,
    nodal_volume,
):
    nearby = fetch_coarse(coarse, n_sub, n_grp)
    block_rows = n_grp * coarse.shape[0]
    offset = (lax.axis_index("sub") - 1) * block_rows
    local_rows = corner_idx[0] - offset
    selector = (local_rows[:, None] == jnp.arange(3 * block_rows, dtype=jnp.int32)[None, :]).astype(
        jnp.float32
    )
    corner_vals = jnp.dot(selector, nearby, precision=lax.Precision.HIGHEST)
    node_count = force.shape[0]
    load_cases = force.shape[2]
    panels = panel_inv.shape[0]
    panel_rows = panel_inv.shape[1]
    correction = jnp.dot(coupling.astype(jnp.float32), corner_vals, precision=lax.Precision.HIGHEST)
    live_mask = jnp.arange(panel_rows)[None, :] < 3 * panel_nodes[0][:, None]
    reduced = (force.reshape(3 * node_count, load_cases).astype(jnp.float32) - correction).reshape(
        panels, panel_rows, load_cases
    )
    reduced = jnp.where(live_mask[:, :, None], reduced, 0.0).astype(jnp.bfloat16)
    solved = jnp.einsum("prc,pcl->prl", panel_inv, reduced, preferred_element_type=jnp.float32)
    displaced = jnp.where(live_mask[:, :, None], solved, 0.0).astype(jnp.bfloat16)
    by_component = (
        displaced.reshape(panels, panel_rows // 3, 3, load_cases)
        .transpose(2, 0, 1, 3)
        .reshape(3, node_count, load_cases)
    )
    elem_count = connect.shape[1]
    node_range = jnp.arange(node_count, dtype=jnp.int32)
    corner_of = (connect.T.reshape(-1)[:, None] == node_range[None, :]).astype(jnp.bfloat16)
    element = jnp.einsum("xn,cnl->xcl", corner_of, by_component, preferred_element_type=jnp.float32)
    element = element.astype(jnp.bfloat16).reshape(elem_count, 24, load_cases)
    strain = jnp.einsum("ije,ejl->eil", strain_disp, element, preferred_element_type=jnp.float32)
    stress = (
        jnp.einsum("ik,ekl->iel", iso_matrix(), strain, precision=lax.Precision.HIGHEST)
        * modulus[None, :, None]
    )
    incidence = jnp.sum(
        (connect[:, None, :] == node_range[None, :, None]).astype(jnp.float32), axis=0
    )
    picker = (interface[0][:, None] == node_range[None, :]).astype(jnp.float32)
    counts = jnp.concatenate([incidence, jnp.dot(picker, incidence)])
    both = jnp.einsum("re,cel->crl", counts, stress, precision=lax.Precision.HIGHEST)
    partial_value = both[:, :node_count]
    added = exchange_faces(both[:, node_count:], n_sub, n_grp)
    summed = partial_value + jnp.einsum(
        "rn,crl->cnl", picker, added, precision=lax.Precision.HIGHEST
    )
    stress_out = (summed / nodal_volume[None, :, None]).astype(jnp.bfloat16).transpose(1, 0, 2)
    return (by_component.transpose(1, 0, 2), stress_out)


def solution(mesh):
    n_sub = mesh.shape["sub"]
    n_grp = mesh.shape["grp"]
    placed = (
        P(("sub", "grp"), None),
        P(("sub", "grp"), None),
        P(("sub", "grp"), None),
        P(("sub", "grp"), None, None),
        P(("sub", "grp"), None, None),
        P(("sub", "grp"), None),
        P(None, None, ("sub", "grp")),
        P(("sub", "grp")),
        P(None, ("sub", "grp")),
        P(("sub", "grp"), None),
        P(("sub", "grp")),
    )
    return jax.shard_map(
        functools.partial(shards, n_sub, n_grp),
        mesh=mesh,
        in_specs=placed,
        out_specs=(P(("sub", "grp"), None, None), P(("sub", "grp"), None, None)),
        check_vma=False,
    )
```

```python
import functools

import jax
import jax.numpy as jnp
import numpy as np
from jax import lax
from jax.experimental import pallas as pl
from jax.experimental.pallas import tpu as pltpu
from jax.sharding import PartitionSpec as P

NIS = 64
NIG = 32
NED = 8

MESH = pl.DeviceIdType.MESH

POISSON = 0.3

SUB_LO = np.arange(0, NIS)
SUB_HI = np.arange(NIS, 2 * NIS)
GRP_LO = np.arange(2 * NIS, 2 * NIS + NIG)
GRP_HI = np.arange(2 * NIS + NIG, 2 * NIS + 2 * NIG)
_E0 = 2 * NIS + 2 * NIG
EDGE_LL = np.arange(_E0, _E0 + NED)
EDGE_LH = np.arange(_E0 + NED, _E0 + 2 * NED)
EDGE_HL = np.arange(_E0 + 2 * NED, _E0 + 3 * NED)
EDGE_HH = np.arange(_E0 + 3 * NED, _E0 + 4 * NED)

DIRECTIONS = (
    (1, 0, (SUB_HI, EDGE_HL, EDGE_HH), (SUB_LO, EDGE_LL, EDGE_LH)),
    (-1, 0, (SUB_LO, EDGE_LL, EDGE_LH), (SUB_HI, EDGE_HL, EDGE_HH)),
    (0, 1, (GRP_HI, EDGE_LH, EDGE_HH), (GRP_LO, EDGE_LL, EDGE_HL)),
    (0, -1, (GRP_LO, EDGE_LL, EDGE_HL), (GRP_HI, EDGE_LH, EDGE_HH)),
    (1, 1, (EDGE_HH,), (EDGE_LL,)),
    (1, -1, (EDGE_HL,), (EDGE_LH,)),
    (-1, 1, (EDGE_LH,), (EDGE_HL,)),
    (-1, -1, (EDGE_LL,), (EDGE_HH,)),
)
SLOT_ROWS = [sum(len(x) for x in d[2]) for d in DIRECTIONS]
SLOT_START = np.concatenate([[0], np.cumsum(SLOT_ROWS)])


def _runs(entries):
    runs = []
    for i in entries:
        if runs and runs[-1][1] == i:
            runs[-1][1] = i + 1
        else:
            runs.append([i, i + 1])
    return [(int(a), int(b)) for a, b in runs]


def _pieces(k, which):
    out = []
    row = int(SLOT_START[k])
    for a, b in _runs(np.concatenate(DIRECTIONS[k][which])):
        out.append((a, b, row))
        row += b - a
    return out


SEND_PIECES = [(k, a, b, row) for k in range(len(DIRECTIONS)) for a, b, row in _pieces(k, 2)]
RECV_PIECES = [_pieces(k, 3) for k in range(len(DIRECTIONS))]


def iso_matrix():
    lame_first = POISSON / ((1.0 + POISSON) * (1.0 - 2.0 * POISSON))
    shear_mod = 0.5 / (1.0 + POISSON)
    elastic = np.zeros((6, 6), np.float32)
    elastic[:3, :3] = lame_first
    elastic[:3, :3] += np.eye(3, dtype=np.float32) * np.float32(2.0 * shear_mod)
    elastic[3:, 3:] = np.eye(3, dtype=np.float32) * np.float32(shear_mod)
    return elastic


def _above(i, n):
    return (i + n - 1) // n


def _below(i, n):
    return (2 * n - 2 - i) // n


def _step_ok(i, d, n):
    if d < 0:
        return _above(i, n)
    if d > 0:
        return _below(i, n)
    return 1


def coarse_kernel(n_sub, n_grp, block_ref, idx_ref, out_ref, buf, send_sem, recv_sem):
    s = lax.axis_index("sub")
    g = lax.axis_index("grp")
    rows = block_ref.shape[0]
    barrier = pltpu.get_barrier_semaphore()

    def peers():
        for ds in (-1, 0, 1):
            for gt in range(n_grp):
                yield ds, gt

    def exists(ds, gt):
        if ds < 0:
            return s + ds >= 0
        if ds > 0:
            return s + ds < n_sub
        return g != gt

    for ds, gt in peers():
        def signal(ds=ds, gt=gt):
            pl.semaphore_signal(barrier, inc=1, device_id=(s + ds, gt), device_id_type=MESH)
        pl.when(exists(ds, gt))(signal)
    count = (n_grp - 1) + n_grp * (_above(s, n_sub) + _below(s, n_sub))
    pl.semaphore_wait(barrier, count)

    copies = []
    for ds, gt in peers():
        slot_there = (1 - ds) * n_grp + g
        copy = pltpu.make_async_remote_copy(
            src_ref=block_ref,
            dst_ref=buf.at[pl.ds(slot_there * rows, rows)],
            send_sem=send_sem.at[(ds + 1) * n_grp + gt],
            recv_sem=recv_sem.at[slot_there],
            device_id=(s + ds, gt),
            device_id_type=MESH,
        )
        pl.when(exists(ds, gt))(copy.start)
        copies.append(copy)
    buf[pl.ds((n_grp + g) * rows, rows), :] = block_ref[...]
    for (ds, gt), copy in zip(peers(), copies):
        pl.when(exists(ds, gt))(copy.wait_send)
    for dr in (-1, 0, 1):
        for gr in range(n_grp):
            slot_here = (dr + 1) * n_grp + gr
            recv = pltpu.make_async_remote_copy(
                src_ref=block_ref,
                dst_ref=buf.at[pl.ds(slot_here * rows, rows)],
                send_sem=send_sem.at[slot_here],
                recv_sem=recv_sem.at[slot_here],
                device_id=(s + dr, gr),
                device_id_type=MESH,
            )
            pl.when(exists(dr, gr))(recv.wait_recv)
    first = (s - 1) * n_grp * rows
    for r in range(idx_ref.shape[1]):
        row = jnp.minimum(jnp.maximum(idx_ref[0, r] - first, 0), buf.shape[0] - 1)
        out_ref[pl.ds(r, 1), :] = buf[pl.ds(row, 1), :]


def face_kernel(n_sub, n_grp, base, send_ref, out_ref, buf, send_sem, recv_sem):
    s = lax.axis_index("sub")
    g = lax.axis_index("grp")
    barrier = pltpu.get_barrier_semaphore()

    def exists(ds, dg):
        conds = []
        if ds < 0:
            conds.append(s + ds >= 0)
        if ds > 0:
            conds.append(s + ds < n_sub)
        if dg < 0:
            conds.append(g + dg >= 0)
        if dg > 0:
            conds.append(g + dg < n_grp)
        cond = conds[0]
        for c in conds[1:]:
            cond = jnp.logical_and(cond, c)
        return cond

    for ds, dg, _, _ in DIRECTIONS:
        def signal(ds=ds, dg=dg):
            pl.semaphore_signal(barrier, inc=1, device_id=(s + ds, g + dg), device_id_type=MESH)
        pl.when(exists(ds, dg))(signal)
    count = 0
    for ds, dg, _, _ in DIRECTIONS:
        count = count + _step_ok(s, ds, n_sub) * _step_ok(g, dg, n_grp)
    pl.semaphore_wait(barrier, count)

    copies = []
    for j, (k, lo, hi, row) in enumerate(SEND_PIECES):
        ds, dg = DIRECTIONS[k][:2]
        copy = pltpu.make_async_remote_copy(
            src_ref=send_ref.at[:, pl.ds(base + lo, hi - lo)],
            dst_ref=buf.at[:, pl.ds(row, hi - lo)],
            send_sem=send_sem.at[j],
            recv_sem=recv_sem.at[j],
            device_id=(s + ds, g + dg),
            device_id_type=MESH,
        )
        pl.when(exists(ds, dg))(copy.start)
        copies.append(copy)
    out_ref[...] = jnp.zeros(out_ref.shape, out_ref.dtype)
    for j, (k, lo, hi, row) in enumerate(SEND_PIECES):
        ds, dg = DIRECTIONS[k][:2]
        pl.when(exists(ds, dg))(copies[j].wait_send)
    for k, (ds, dg, _, _) in enumerate(DIRECTIONS):
        mine = [j for j, piece in enumerate(SEND_PIECES) if piece[0] == k]

        def take(k=k, mine=mine):
            for j in mine:
                copies[j].wait_recv()
            for lo, hi, row in RECV_PIECES[k]:
                out_ref[:, lo:hi, :] += buf[:, row:row + hi - lo, :]

        pl.when(exists(-ds, -dg))(take)


def fetch_corners(block, corner_idx, n_sub, n_grp):
    rows, width = block.shape
    slots = 3 * n_grp
    return pl.pallas_call(
        functools.partial(coarse_kernel, n_sub, n_grp),
        out_shape=jax.ShapeDtypeStruct((corner_idx.shape[1], width), block.dtype),
        in_specs=[
            pl.BlockSpec(memory_space=pltpu.VMEM),
            pl.BlockSpec(memory_space=pltpu.SMEM),
        ],
        out_specs=pl.BlockSpec(memory_space=pltpu.VMEM),
        scratch_shapes=[
            pltpu.VMEM((slots * rows, width), block.dtype),
            pltpu.SemaphoreType.DMA((slots,)),
            pltpu.SemaphoreType.DMA((slots,)),
        ],
        compiler_params=pltpu.CompilerParams(collective_id=0, has_side_effects=True),
    )(block, corner_idx)


def exchange_faces(send, base, n_sub, n_grp):
    return pl.pallas_call(
        functools.partial(face_kernel, n_sub, n_grp, base),
        out_shape=jax.ShapeDtypeStruct(
            (send.shape[0], send.shape[1] - base, send.shape[2]), send.dtype
        ),
        in_specs=[pl.BlockSpec(memory_space=pltpu.VMEM)],
        out_specs=pl.BlockSpec(memory_space=pltpu.VMEM),
        scratch_shapes=[
            pltpu.VMEM((send.shape[0], int(SLOT_START[-1]), send.shape[2]), send.dtype),
            pltpu.SemaphoreType.DMA((len(SEND_PIECES),)),
            pltpu.SemaphoreType.DMA((len(SEND_PIECES),)),
        ],
        compiler_params=pltpu.CompilerParams(collective_id=1, has_side_effects=True),
    )(send)


def shards(
    n_sub,
    n_grp,
    coarse,
    corner_idx,
    coupling,
    force,
    panel_inv,
    panel_nodes,
    strain_disp,
    modulus,
    connect,
    interface,
    nodal_volume,
):
    corner_vals = fetch_corners(coarse, corner_idx, n_sub, n_grp)
    node_count = force.shape[0]
    load_cases = force.shape[2]
    panels = panel_inv.shape[0]
    panel_rows = panel_inv.shape[1]
    correction = jnp.dot(coupling.astype(jnp.float32), corner_vals, precision=lax.Precision.HIGHEST)
    live_mask = jnp.arange(panel_rows)[None, :] < 3 * panel_nodes[0][:, None]
    reduced = (force.reshape(3 * node_count, load_cases).astype(jnp.float32) - correction).reshape(
        panels, panel_rows, load_cases
    )
    reduced = jnp.where(live_mask[:, :, None], reduced, 0.0).astype(jnp.bfloat16)
    solved = jnp.einsum("prc,pcl->prl", panel_inv, reduced, preferred_element_type=jnp.float32)
    displaced = jnp.where(live_mask[:, :, None], solved, 0.0).astype(jnp.bfloat16)
    by_component = (
        displaced.reshape(panels, panel_rows // 3, 3, load_cases)
        .transpose(2, 0, 1, 3)
        .reshape(3, node_count, load_cases)
    )
    elem_count = connect.shape[1]
    node_range = jnp.arange(node_count, dtype=jnp.int32)
    corner_of = (connect.T.reshape(-1)[:, None] == node_range[None, :]).astype(jnp.bfloat16)
    element = jnp.einsum("xn,cnl->xcl", corner_of, by_component, preferred_element_type=jnp.float32)
    element = element.astype(jnp.bfloat16).reshape(elem_count, 24, load_cases)
    strain = jnp.einsum("ije,ejl->eil", strain_disp, element, preferred_element_type=jnp.float32)
    stress = (
        jnp.einsum("ik,ekl->iel", iso_matrix(), strain, precision=lax.Precision.HIGHEST)
        * modulus[None, :, None]
    )
    incidence = jnp.sum(
        (connect[:, None, :] == node_range[None, :, None]).astype(jnp.float32), axis=0
    )
    picker = (interface[0][:, None] == node_range[None, :]).astype(jnp.float32)
    counts = jnp.concatenate([incidence, jnp.dot(picker, incidence)])
    both = jnp.einsum("re,cel->crl", counts, stress, precision=lax.Precision.HIGHEST)
    partial_value = both[:, :node_count]
    added = exchange_faces(both, node_count, n_sub, n_grp)
    summed = partial_value + jnp.einsum(
        "rn,crl->cnl", picker, added, precision=lax.Precision.HIGHEST
    )
    stress_out = (summed / nodal_volume[None, :, None]).astype(jnp.bfloat16).transpose(1, 0, 2)
    return (by_component.transpose(1, 0, 2), stress_out)


def solution(mesh):
    n_sub = mesh.shape["sub"]
    n_grp = mesh.shape["grp"]
    placed = (
        P(("sub", "grp"), None),
        P(("sub", "grp"), None),
        P(("sub", "grp"), None),
        P(("sub", "grp"), None, None),
        P(("sub", "grp"), None, None),
        P(("sub", "grp"), None),
        P(None, None, ("sub", "grp")),
        P(("sub", "grp")),
        P(None, ("sub", "grp")),
        P(("sub", "grp"), None),
        P(("sub", "grp")),
    )
    return jax.shard_map(
        functools.partial(shards, n_sub, n_grp),
        mesh=mesh,
        in_specs=placed,
        out_specs=(P(("sub", "grp"), None, None), P(("sub", "grp"), None, None)),
        check_vma=False,
    )
```

```python
import functools

import jax
import jax.numpy as jnp
import numpy as np
from jax import lax
from jax.experimental import pallas as pl
from jax.experimental.pallas import tpu as pltpu
from jax.sharding import PartitionSpec as P

NIS = 64
NIG = 32
NED = 8

MESH = pl.DeviceIdType.MESH

POISSON = 0.3

SUB_LO = np.arange(0, NIS)
SUB_HI = np.arange(NIS, 2 * NIS)
GRP_LO = np.arange(2 * NIS, 2 * NIS + NIG)
GRP_HI = np.arange(2 * NIS + NIG, 2 * NIS + 2 * NIG)
_E0 = 2 * NIS + 2 * NIG
EDGE_LL = np.arange(_E0, _E0 + NED)
EDGE_LH = np.arange(_E0 + NED, _E0 + 2 * NED)
EDGE_HL = np.arange(_E0 + 2 * NED, _E0 + 3 * NED)
EDGE_HH = np.arange(_E0 + 3 * NED, _E0 + 4 * NED)

DIRECTIONS = (
    (1, 0, (SUB_HI, EDGE_HL, EDGE_HH), (SUB_LO, EDGE_LL, EDGE_LH)),
    (-1, 0, (SUB_LO, EDGE_LL, EDGE_LH), (SUB_HI, EDGE_HL, EDGE_HH)),
    (0, 1, (GRP_HI, EDGE_LH, EDGE_HH), (GRP_LO, EDGE_LL, EDGE_HL)),
    (0, -1, (GRP_LO, EDGE_LL, EDGE_HL), (GRP_HI, EDGE_LH, EDGE_HH)),
    (1, 1, (EDGE_HH,), (EDGE_LL,)),
    (1, -1, (EDGE_HL,), (EDGE_LH,)),
    (-1, 1, (EDGE_LH,), (EDGE_HL,)),
    (-1, -1, (EDGE_LL,), (EDGE_HH,)),
)
SLOT_ROWS = [sum(len(x) for x in d[2]) for d in DIRECTIONS]
SLOT_START = np.concatenate([[0], np.cumsum(SLOT_ROWS)])


def _runs(entries):
    runs = []
    for i in entries:
        if runs and runs[-1][1] == i:
            runs[-1][1] = i + 1
        else:
            runs.append([i, i + 1])
    return [(int(a), int(b)) for a, b in runs]


def _pieces(k, which):
    out = []
    row = int(SLOT_START[k])
    for a, b in _runs(np.concatenate(DIRECTIONS[k][which])):
        out.append((a, b, row))
        row += b - a
    return out


SEND_PIECES = [(k, a, b, row) for k in range(len(DIRECTIONS)) for a, b, row in _pieces(k, 2)]
RECV_PIECES = [_pieces(k, 3) for k in range(len(DIRECTIONS))]


def iso_matrix():
    lame_first = POISSON / ((1.0 + POISSON) * (1.0 - 2.0 * POISSON))
    shear_mod = 0.5 / (1.0 + POISSON)
    elastic = np.zeros((6, 6), np.float32)
    elastic[:3, :3] = lame_first
    elastic[:3, :3] += np.eye(3, dtype=np.float32) * np.float32(2.0 * shear_mod)
    elastic[3:, 3:] = np.eye(3, dtype=np.float32) * np.float32(shear_mod)
    return elastic


def _above(i, n):
    return (i + n - 1) // n


def _below(i, n):
    return (2 * n - 2 - i) // n


def _step_ok(i, d, n):
    if d < 0:
        return _above(i, n)
    if d > 0:
        return _below(i, n)
    return 1


def coarse_kernel(n_sub, n_grp, block_ref, idx_ref, out_ref, buf, send_sem, recv_sem):
    s = lax.axis_index("sub")
    g = lax.axis_index("grp")
    rows = block_ref.shape[0]
    barrier = pltpu.get_barrier_semaphore()

    def peers():
        for ds in (-1, 0, 1):
            for gt in range(n_grp):
                yield ds, gt

    def exists(ds, gt):
        if ds < 0:
            return s + ds >= 0
        if ds > 0:
            return s + ds < n_sub
        return g != gt

    for ds, gt in peers():
        def signal(ds=ds, gt=gt):
            pl.semaphore_signal(barrier, inc=1, device_id=(s + ds, gt), device_id_type=MESH)
        pl.when(exists(ds, gt))(signal)
    count = (n_grp - 1) + n_grp * (_above(s, n_sub) + _below(s, n_sub))
    pl.semaphore_wait(barrier, count)

    copies = []
    for ds, gt in peers():
        slot_there = (1 - ds) * n_grp + g
        copy = pltpu.make_async_remote_copy(
            src_ref=block_ref,
            dst_ref=buf.at[pl.ds(slot_there * rows, rows)],
            send_sem=send_sem.at[(ds + 1) * n_grp + gt],
            recv_sem=recv_sem.at[slot_there],
            device_id=(s + ds, gt),
            device_id_type=MESH,
        )
        pl.when(exists(ds, gt))(copy.start)
        copies.append(copy)
    buf[pl.ds((n_grp + g) * rows, rows), :] = block_ref[...]
    for (ds, gt), copy in zip(peers(), copies):
        pl.when(exists(ds, gt))(copy.wait_send)
    for dr in (-1, 0, 1):
        for gr in range(n_grp):
            slot_here = (dr + 1) * n_grp + gr
            recv = pltpu.make_async_remote_copy(
                src_ref=block_ref,
                dst_ref=buf.at[pl.ds(slot_here * rows, rows)],
                send_sem=send_sem.at[slot_here],
                recv_sem=recv_sem.at[slot_here],
                device_id=(s + dr, gr),
                device_id_type=MESH,
            )
            pl.when(exists(dr, gr))(recv.wait_recv)
    first = (s - 1) * n_grp * rows
    for r in range(idx_ref.shape[1]):
        row = jnp.minimum(jnp.maximum(idx_ref[0, r] - first, 0), buf.shape[0] - 1)
        out_ref[pl.ds(r, 1), :] = buf[pl.ds(row, 1), :]


def face_kernel(
    n_sub, n_grp, send_ref, stress_ref, own_ref, spread_ref, out_ref, buf, added, acc, send_sem, recv_sem
):
    s = lax.axis_index("sub")
    g = lax.axis_index("grp")
    barrier = pltpu.get_barrier_semaphore()

    def exists(ds, dg):
        conds = []
        if ds < 0:
            conds.append(s + ds >= 0)
        if ds > 0:
            conds.append(s + ds < n_sub)
        if dg < 0:
            conds.append(g + dg >= 0)
        if dg > 0:
            conds.append(g + dg < n_grp)
        cond = conds[0]
        for c in conds[1:]:
            cond = jnp.logical_and(cond, c)
        return cond

    for ds, dg, _, _ in DIRECTIONS:
        def signal(ds=ds, dg=dg):
            pl.semaphore_signal(barrier, inc=1, device_id=(s + ds, g + dg), device_id_type=MESH)
        pl.when(exists(ds, dg))(signal)
    count = 0
    for ds, dg, _, _ in DIRECTIONS:
        count = count + _step_ok(s, ds, n_sub) * _step_ok(g, dg, n_grp)
    pl.semaphore_wait(barrier, count)

    copies = []
    for j, (k, lo, hi, row) in enumerate(SEND_PIECES):
        ds, dg = DIRECTIONS[k][:2]
        copy = pltpu.make_async_remote_copy(
            src_ref=send_ref.at[:, pl.ds(lo, hi - lo)],
            dst_ref=buf.at[:, pl.ds(row, hi - lo)],
            send_sem=send_sem.at[j],
            recv_sem=recv_sem.at[j],
            device_id=(s + ds, g + dg),
            device_id_type=MESH,
        )
        pl.when(exists(ds, dg))(copy.start)
        copies.append(copy)
    added[...] = jnp.zeros(added.shape, added.dtype)
    for c in range(acc.shape[0]):
        acc[c] = jnp.dot(
            own_ref[...], stress_ref[c], precision=lax.Precision.HIGHEST,
            preferred_element_type=jnp.float32,
        )
    for j, (k, lo, hi, row) in enumerate(SEND_PIECES):
        ds, dg = DIRECTIONS[k][:2]
        pl.when(exists(ds, dg))(copies[j].wait_send)
    for k, (ds, dg, _, _) in enumerate(DIRECTIONS):
        mine = [j for j, piece in enumerate(SEND_PIECES) if piece[0] == k]

        def take(k=k, mine=mine):
            for j in mine:
                copies[j].wait_recv()
            for lo, hi, row in RECV_PIECES[k]:
                added[:, lo:hi, :] += buf[:, row:row + hi - lo, :]

        pl.when(exists(-ds, -dg))(take)
    for c in range(acc.shape[0]):
        total = acc[c] + jnp.dot(
            spread_ref[...], added[c], precision=lax.Precision.HIGHEST,
            preferred_element_type=jnp.float32,
        )
        out_ref[c] = total.astype(out_ref.dtype)


def fetch_corners(block, corner_idx, n_sub, n_grp):
    rows, width = block.shape
    slots = 3 * n_grp
    return pl.pallas_call(
        functools.partial(coarse_kernel, n_sub, n_grp),
        out_shape=jax.ShapeDtypeStruct((corner_idx.shape[1], width), block.dtype),
        in_specs=[
            pl.BlockSpec(memory_space=pltpu.VMEM),
            pl.BlockSpec(memory_space=pltpu.SMEM),
        ],
        out_specs=pl.BlockSpec(memory_space=pltpu.VMEM),
        scratch_shapes=[
            pltpu.VMEM((slots * rows, width), block.dtype),
            pltpu.SemaphoreType.DMA((slots,)),
            pltpu.SemaphoreType.DMA((slots,)),
        ],
        compiler_params=pltpu.CompilerParams(collective_id=0, has_side_effects=True),
    )(block, corner_idx)


def exchange_faces(send, stress, own, spread, n_sub, n_grp):
    parts, nodes = stress.shape[0], own.shape[0]
    return pl.pallas_call(
        functools.partial(face_kernel, n_sub, n_grp),
        out_shape=jax.ShapeDtypeStruct((parts, nodes, send.shape[2]), jnp.bfloat16),
        in_specs=[pl.BlockSpec(memory_space=pltpu.VMEM)] * 4,
        out_specs=pl.BlockSpec(memory_space=pltpu.VMEM),
        scratch_shapes=[
            pltpu.VMEM((send.shape[0], int(SLOT_START[-1]), send.shape[2]), send.dtype),
            pltpu.VMEM(send.shape, send.dtype),
            pltpu.VMEM((parts, nodes, send.shape[2]), jnp.float32),
            pltpu.SemaphoreType.DMA((len(SEND_PIECES),)),
            pltpu.SemaphoreType.DMA((len(SEND_PIECES),)),
        ],
        compiler_params=pltpu.CompilerParams(collective_id=1, has_side_effects=True),
    )(send, stress, own, spread)


def shards(
    n_sub,
    n_grp,
    coarse,
    corner_idx,
    coupling,
    force,
    panel_inv,
    panel_nodes,
    strain_disp,
    modulus,
    connect,
    interface,
    nodal_volume,
):
    corner_vals = fetch_corners(coarse, corner_idx, n_sub, n_grp)
    node_count = force.shape[0]
    load_cases = force.shape[2]
    panels = panel_inv.shape[0]
    panel_rows = panel_inv.shape[1]
    correction = jnp.dot(coupling.astype(jnp.float32), corner_vals, precision=lax.Precision.HIGHEST)
    live_mask = jnp.arange(panel_rows)[None, :] < 3 * panel_nodes[0][:, None]
    reduced = (force.reshape(3 * node_count, load_cases).astype(jnp.float32) - correction).reshape(
        panels, panel_rows, load_cases
    )
    reduced = jnp.where(live_mask[:, :, None], reduced, 0.0).astype(jnp.bfloat16)
    solved = jnp.einsum("prc,pcl->prl", panel_inv, reduced, preferred_element_type=jnp.float32)
    displaced = jnp.where(live_mask[:, :, None], solved, 0.0).astype(jnp.bfloat16)
    by_component = (
        displaced.reshape(panels, panel_rows // 3, 3, load_cases)
        .transpose(2, 0, 1, 3)
        .reshape(3, node_count, load_cases)
    )
    elem_count = connect.shape[1]
    node_range = jnp.arange(node_count, dtype=jnp.int32)
    corner_of = (connect.T.reshape(-1)[:, None] == node_range[None, :]).astype(jnp.bfloat16)
    element = jnp.einsum("xn,cnl->xcl", corner_of, by_component, preferred_element_type=jnp.float32)
    element = element.astype(jnp.bfloat16).reshape(elem_count, 24, load_cases)
    strain = jnp.einsum("ije,ejl->eil", strain_disp, element, preferred_element_type=jnp.float32)
    stress = (
        jnp.einsum("ik,ekl->iel", iso_matrix(), strain, precision=lax.Precision.HIGHEST)
        * modulus[None, :, None]
    )
    incidence = jnp.sum(
        (connect[:, None, :] == node_range[None, :, None]).astype(jnp.float32), axis=0
    )
    picker = (interface[0][:, None] == node_range[None, :]).astype(jnp.float32)
    send = jnp.einsum(
        "re,cel->crl", jnp.dot(picker, incidence), stress, precision=lax.Precision.HIGHEST
    )
    inverse_volume = 1.0 / nodal_volume
    own = incidence * inverse_volume[:, None]
    spread = picker.T * inverse_volume[:, None]
    stress_out = exchange_faces(send, stress, own, spread, n_sub, n_grp).transpose(1, 0, 2)
    return (by_component.transpose(1, 0, 2), stress_out)


def solution(mesh):
    n_sub = mesh.shape["sub"]
    n_grp = mesh.shape["grp"]
    placed = (
        P(("sub", "grp"), None),
        P(("sub", "grp"), None),
        P(("sub", "grp"), None),
        P(("sub", "grp"), None, None),
        P(("sub", "grp"), None, None),
        P(("sub", "grp"), None),
        P(None, None, ("sub", "grp")),
        P(("sub", "grp")),
        P(None, ("sub", "grp")),
        P(("sub", "grp"), None),
        P(("sub", "grp")),
    )
    return jax.shard_map(
        functools.partial(shards, n_sub, n_grp),
        mesh=mesh,
        in_specs=placed,
        out_specs=(P(("sub", "grp"), None, None), P(("sub", "grp"), None, None)),
        check_vma=False,
    )
```

```python
import functools

import jax
import jax.numpy as jnp
import numpy as np
from jax import lax
from jax.experimental import pallas as pl
from jax.experimental.pallas import tpu as pltpu
from jax.sharding import PartitionSpec as P

NIS = 64
NIG = 32
NED = 8

MESH = pl.DeviceIdType.MESH

POISSON = 0.3

SUB_LO = np.arange(0, NIS)
SUB_HI = np.arange(NIS, 2 * NIS)
GRP_LO = np.arange(2 * NIS, 2 * NIS + NIG)
GRP_HI = np.arange(2 * NIS + NIG, 2 * NIS + 2 * NIG)
_E0 = 2 * NIS + 2 * NIG
EDGE_LL = np.arange(_E0, _E0 + NED)
EDGE_LH = np.arange(_E0 + NED, _E0 + 2 * NED)
EDGE_HL = np.arange(_E0 + 2 * NED, _E0 + 3 * NED)
EDGE_HH = np.arange(_E0 + 3 * NED, _E0 + 4 * NED)

DIRECTIONS = (
    (1, 0, (SUB_HI, EDGE_HL, EDGE_HH), (SUB_LO, EDGE_LL, EDGE_LH)),
    (-1, 0, (SUB_LO, EDGE_LL, EDGE_LH), (SUB_HI, EDGE_HL, EDGE_HH)),
    (0, 1, (GRP_HI, EDGE_LH, EDGE_HH), (GRP_LO, EDGE_LL, EDGE_HL)),
    (0, -1, (GRP_LO, EDGE_LL, EDGE_HL), (GRP_HI, EDGE_LH, EDGE_HH)),
    (1, 1, (EDGE_HH,), (EDGE_LL,)),
    (1, -1, (EDGE_HL,), (EDGE_LH,)),
    (-1, 1, (EDGE_LH,), (EDGE_HL,)),
    (-1, -1, (EDGE_LL,), (EDGE_HH,)),
)
SLOT_ROWS = [sum(len(x) for x in d[2]) for d in DIRECTIONS]
SLOT_START = np.concatenate([[0], np.cumsum(SLOT_ROWS)])


def _runs(entries):
    runs = []
    for i in entries:
        if runs and runs[-1][1] == i:
            runs[-1][1] = i + 1
        else:
            runs.append([i, i + 1])
    return [(int(a), int(b)) for a, b in runs]


def _pieces(k, which):
    out = []
    row = int(SLOT_START[k])
    for a, b in _runs(np.concatenate(DIRECTIONS[k][which])):
        out.append((a, b, row))
        row += b - a
    return out


SEND_PIECES = [(k, a, b, row) for k in range(len(DIRECTIONS)) for a, b, row in _pieces(k, 2)]
RECV_PIECES = [_pieces(k, 3) for k in range(len(DIRECTIONS))]


def iso_matrix():
    lame_first = POISSON / ((1.0 + POISSON) * (1.0 - 2.0 * POISSON))
    shear_mod = 0.5 / (1.0 + POISSON)
    elastic = np.zeros((6, 6), np.float32)
    elastic[:3, :3] = lame_first
    elastic[:3, :3] += np.eye(3, dtype=np.float32) * np.float32(2.0 * shear_mod)
    elastic[3:, 3:] = np.eye(3, dtype=np.float32) * np.float32(shear_mod)
    return elastic


def _above(i, n):
    return (i + n - 1) // n


def _below(i, n):
    return (2 * n - 2 - i) // n


def _step_ok(i, d, n):
    if d < 0:
        return _above(i, n)
    if d > 0:
        return _below(i, n)
    return 1


def coarse_kernel(n_sub, n_grp, block_ref, idx_ref, out_ref, buf, send_sem, recv_sem):
    s = lax.axis_index("sub")
    g = lax.axis_index("grp")
    rows = block_ref.shape[0]
    barrier = pltpu.get_barrier_semaphore()

    def peers():
        for ds in (-1, 0, 1):
            for gt in range(n_grp):
                yield ds, gt

    def exists(ds, gt):
        if ds < 0:
            return s + ds >= 0
        if ds > 0:
            return s + ds < n_sub
        return g != gt

    for ds, gt in peers():
        def signal(ds=ds, gt=gt):
            pl.semaphore_signal(barrier, inc=1, device_id=(s + ds, gt), device_id_type=MESH)
        pl.when(exists(ds, gt))(signal)
    count = (n_grp - 1) + n_grp * (_above(s, n_sub) + _below(s, n_sub))
    pl.semaphore_wait(barrier, count)

    copies = []
    for ds, gt in peers():
        slot_there = (1 - ds) * n_grp + g
        copy = pltpu.make_async_remote_copy(
            src_ref=block_ref,
            dst_ref=buf.at[pl.ds(slot_there * rows, rows)],
            send_sem=send_sem.at[(ds + 1) * n_grp + gt],
            recv_sem=recv_sem.at[slot_there],
            device_id=(s + ds, gt),
            device_id_type=MESH,
        )
        pl.when(exists(ds, gt))(copy.start)
        copies.append(copy)
    buf[pl.ds((n_grp + g) * rows, rows), :] = block_ref[...]
    for (ds, gt), copy in zip(peers(), copies):
        pl.when(exists(ds, gt))(copy.wait_send)
    for dr in (-1, 0, 1):
        for gr in range(n_grp):
            slot_here = (dr + 1) * n_grp + gr
            recv = pltpu.make_async_remote_copy(
                src_ref=block_ref,
                dst_ref=buf.at[pl.ds(slot_here * rows, rows)],
                send_sem=send_sem.at[slot_here],
                recv_sem=recv_sem.at[slot_here],
                device_id=(s + dr, gr),
                device_id_type=MESH,
            )
            pl.when(exists(dr, gr))(recv.wait_recv)
    first = (s - 1) * n_grp * rows
    for r in range(idx_ref.shape[1]):
        row = jnp.minimum(jnp.maximum(idx_ref[0, r] - first, 0), buf.shape[0] - 1)
        out_ref[pl.ds(r, 1), :] = buf[pl.ds(row, 1), :]


def face_kernel(
    n_sub, n_grp, send_ref, stress_ref, own_ref, spread_ref, out_ref, buf, added, acc, send_sem, recv_sem
):
    s = lax.axis_index("sub")
    g = lax.axis_index("grp")
    barrier = pltpu.get_barrier_semaphore()

    def exists(ds, dg):
        conds = []
        if ds < 0:
            conds.append(s + ds >= 0)
        if ds > 0:
            conds.append(s + ds < n_sub)
        if dg < 0:
            conds.append(g + dg >= 0)
        if dg > 0:
            conds.append(g + dg < n_grp)
        cond = conds[0]
        for c in conds[1:]:
            cond = jnp.logical_and(cond, c)
        return cond

    for ds, dg, _, _ in DIRECTIONS:
        def signal(ds=ds, dg=dg):
            pl.semaphore_signal(barrier, inc=1, device_id=(s + ds, g + dg), device_id_type=MESH)
        pl.when(exists(ds, dg))(signal)
    count = 0
    for ds, dg, _, _ in DIRECTIONS:
        count = count + _step_ok(s, ds, n_sub) * _step_ok(g, dg, n_grp)
    pl.semaphore_wait(barrier, count)

    copies = []
    for j, (k, lo, hi, row) in enumerate(SEND_PIECES):
        ds, dg = DIRECTIONS[k][:2]
        copy = pltpu.make_async_remote_copy(
            src_ref=send_ref.at[:, pl.ds(lo, hi - lo)],
            dst_ref=buf.at[:, pl.ds(row, hi - lo)],
            send_sem=send_sem.at[j],
            recv_sem=recv_sem.at[j],
            device_id=(s + ds, g + dg),
            device_id_type=MESH,
        )
        pl.when(exists(ds, dg))(copy.start)
        copies.append(copy)
    added[...] = jnp.zeros(added.shape, added.dtype)
    for c in range(acc.shape[0]):
        acc[c] = jnp.dot(
            own_ref[...], stress_ref[c], precision=lax.Precision.HIGHEST,
            preferred_element_type=jnp.float32,
        )
    for j, (k, lo, hi, row) in enumerate(SEND_PIECES):
        ds, dg = DIRECTIONS[k][:2]
        pl.when(exists(ds, dg))(copies[j].wait_send)
    for k, (ds, dg, _, _) in enumerate(DIRECTIONS):
        mine = [j for j, piece in enumerate(SEND_PIECES) if piece[0] == k]

        def take(k=k, mine=mine):
            for j in mine:
                copies[j].wait_recv()
            for lo, hi, row in RECV_PIECES[k]:
                added[:, lo:hi, :] += buf[:, row:row + hi - lo, :]

        pl.when(exists(-ds, -dg))(take)
    for c in range(acc.shape[0]):
        total = acc[c] + jnp.dot(
            spread_ref[...], added[c], precision=lax.Precision.HIGHEST,
            preferred_element_type=jnp.float32,
        )
        out_ref[c] = total.astype(out_ref.dtype)


def fetch_corners(block, corner_idx, n_sub, n_grp):
    rows, width = block.shape
    slots = 3 * n_grp
    return pl.pallas_call(
        functools.partial(coarse_kernel, n_sub, n_grp),
        out_shape=jax.ShapeDtypeStruct((corner_idx.shape[1], width), block.dtype),
        in_specs=[
            pl.BlockSpec(memory_space=pltpu.VMEM),
            pl.BlockSpec(memory_space=pltpu.SMEM),
        ],
        out_specs=pl.BlockSpec(memory_space=pltpu.VMEM),
        scratch_shapes=[
            pltpu.VMEM((slots * rows, width), block.dtype),
            pltpu.SemaphoreType.DMA((slots,)),
            pltpu.SemaphoreType.DMA((slots,)),
        ],
        compiler_params=pltpu.CompilerParams(collective_id=0, has_side_effects=True),
    )(block, corner_idx)


def exchange_faces(send, stress, own, spread, n_sub, n_grp):
    parts, nodes = stress.shape[0], own.shape[0]
    return pl.pallas_call(
        functools.partial(face_kernel, n_sub, n_grp),
        out_shape=jax.ShapeDtypeStruct((parts, nodes, send.shape[2]), jnp.float32),
        in_specs=[pl.BlockSpec(memory_space=pltpu.VMEM)] * 4,
        out_specs=pl.BlockSpec(memory_space=pltpu.VMEM),
        scratch_shapes=[
            pltpu.VMEM((send.shape[0], int(SLOT_START[-1]), send.shape[2]), send.dtype),
            pltpu.VMEM(send.shape, send.dtype),
            pltpu.VMEM((parts, nodes, send.shape[2]), jnp.float32),
            pltpu.SemaphoreType.DMA((len(SEND_PIECES),)),
            pltpu.SemaphoreType.DMA((len(SEND_PIECES),)),
        ],
        compiler_params=pltpu.CompilerParams(collective_id=1, has_side_effects=True),
    )(send, stress, own, spread)


def shards(
    n_sub,
    n_grp,
    coarse,
    corner_idx,
    coupling,
    force,
    panel_inv,
    panel_nodes,
    strain_disp,
    modulus,
    connect,
    interface,
    nodal_volume,
):
    corner_vals = fetch_corners(coarse, corner_idx, n_sub, n_grp)
    node_count = force.shape[0]
    load_cases = force.shape[2]
    panels = panel_inv.shape[0]
    panel_rows = panel_inv.shape[1]
    correction = jnp.dot(coupling.astype(jnp.float32), corner_vals, precision=lax.Precision.HIGHEST)
    live_mask = jnp.arange(panel_rows)[None, :] < 3 * panel_nodes[0][:, None]
    reduced = (force.reshape(3 * node_count, load_cases).astype(jnp.float32) - correction).reshape(
        panels, panel_rows, load_cases
    )
    reduced = jnp.where(live_mask[:, :, None], reduced, 0.0).astype(jnp.bfloat16)
    solved = jnp.einsum("prc,pcl->prl", panel_inv, reduced, preferred_element_type=jnp.float32)
    displaced = jnp.where(live_mask[:, :, None], solved, 0.0).astype(jnp.bfloat16)
    by_component = (
        displaced.reshape(panels, panel_rows // 3, 3, load_cases)
        .transpose(2, 0, 1, 3)
        .reshape(3, node_count, load_cases)
    )
    elem_count = connect.shape[1]
    node_range = jnp.arange(node_count, dtype=jnp.int32)
    corner_of = (connect.T.reshape(-1)[:, None] == node_range[None, :]).astype(jnp.bfloat16)
    element = jnp.einsum("xn,cnl->xcl", corner_of, by_component, preferred_element_type=jnp.float32)
    element = element.astype(jnp.bfloat16).reshape(elem_count, 24, load_cases)
    strain = jnp.einsum("ije,ejl->eil", strain_disp, element, preferred_element_type=jnp.float32)
    stress = (
        jnp.einsum("ik,ekl->iel", iso_matrix(), strain, precision=lax.Precision.HIGHEST)
        * modulus[None, :, None]
    )
    incidence = jnp.sum(
        (connect[:, None, :] == node_range[None, :, None]).astype(jnp.float32), axis=0
    )
    picker = (interface[0][:, None] == node_range[None, :]).astype(jnp.float32)
    send = jnp.einsum(
        "re,cel->crl", jnp.dot(picker, incidence), stress, precision=lax.Precision.HIGHEST
    )
    inverse_volume = 1.0 / nodal_volume
    own = incidence * inverse_volume[:, None]
    spread = picker.T * inverse_volume[:, None]
    stress_out = exchange_faces(send, stress, own, spread, n_sub, n_grp)
    stress_out = stress_out.astype(jnp.bfloat16).transpose(1, 0, 2)
    return (by_component.transpose(1, 0, 2), stress_out)


def solution(mesh):
    n_sub = mesh.shape["sub"]
    n_grp = mesh.shape["grp"]
    placed = (
        P(("sub", "grp"), None),
        P(("sub", "grp"), None),
        P(("sub", "grp"), None),
        P(("sub", "grp"), None, None),
        P(("sub", "grp"), None, None),
        P(("sub", "grp"), None),
        P(None, None, ("sub", "grp")),
        P(("sub", "grp")),
        P(None, ("sub", "grp")),
        P(("sub", "grp"), None),
        P(("sub", "grp")),
    )
    return jax.shard_map(
        functools.partial(shards, n_sub, n_grp),
        mesh=mesh,
        in_specs=placed,
        out_specs=(P(("sub", "grp"), None, None), P(("sub", "grp"), None, None)),
        check_vma=False,
    )
```

```python
import functools

import jax
import jax.numpy as jnp
import numpy as np
from jax import lax
from jax.experimental import pallas as pl
from jax.experimental.pallas import tpu as pltpu
from jax.sharding import PartitionSpec as P

NIS = 64
NIG = 32
NED = 8

MESH = pl.DeviceIdType.MESH

POISSON = 0.3

SUB_LO = np.arange(0, NIS)
SUB_HI = np.arange(NIS, 2 * NIS)
GRP_LO = np.arange(2 * NIS, 2 * NIS + NIG)
GRP_HI = np.arange(2 * NIS + NIG, 2 * NIS + 2 * NIG)
_E0 = 2 * NIS + 2 * NIG
EDGE_LL = np.arange(_E0, _E0 + NED)
EDGE_LH = np.arange(_E0 + NED, _E0 + 2 * NED)
EDGE_HL = np.arange(_E0 + 2 * NED, _E0 + 3 * NED)
EDGE_HH = np.arange(_E0 + 3 * NED, _E0 + 4 * NED)

DIRECTIONS = (
    (1, 0, (SUB_HI, EDGE_HL, EDGE_HH), (SUB_LO, EDGE_LL, EDGE_LH)),
    (-1, 0, (SUB_LO, EDGE_LL, EDGE_LH), (SUB_HI, EDGE_HL, EDGE_HH)),
    (0, 1, (GRP_HI, EDGE_LH, EDGE_HH), (GRP_LO, EDGE_LL, EDGE_HL)),
    (0, -1, (GRP_LO, EDGE_LL, EDGE_HL), (GRP_HI, EDGE_LH, EDGE_HH)),
    (1, 1, (EDGE_HH,), (EDGE_LL,)),
    (1, -1, (EDGE_HL,), (EDGE_LH,)),
    (-1, 1, (EDGE_LH,), (EDGE_HL,)),
    (-1, -1, (EDGE_LL,), (EDGE_HH,)),
)
SLOT_ROWS = [sum(len(x) for x in d[2]) for d in DIRECTIONS]
SLOT_START = np.concatenate([[0], np.cumsum(SLOT_ROWS)])


def _runs(entries):
    runs = []
    for i in entries:
        if runs and runs[-1][1] == i:
            runs[-1][1] = i + 1
        else:
            runs.append([i, i + 1])
    return [(int(a), int(b)) for a, b in runs]


def _pieces(k, which):
    out = []
    row = int(SLOT_START[k])
    for a, b in _runs(np.concatenate(DIRECTIONS[k][which])):
        out.append((a, b, row))
        row += b - a
    return out


SEND_PIECES = [(k, a, b, row) for k in range(len(DIRECTIONS)) for a, b, row in _pieces(k, 2)]
RECV_PIECES = [_pieces(k, 3) for k in range(len(DIRECTIONS))]


def iso_matrix():
    lame_first = POISSON / ((1.0 + POISSON) * (1.0 - 2.0 * POISSON))
    shear_mod = 0.5 / (1.0 + POISSON)
    elastic = np.zeros((6, 6), np.float32)
    elastic[:3, :3] = lame_first
    elastic[:3, :3] += np.eye(3, dtype=np.float32) * np.float32(2.0 * shear_mod)
    elastic[3:, 3:] = np.eye(3, dtype=np.float32) * np.float32(shear_mod)
    return elastic


def _above(i, n):
    return (i + n - 1) // n


def _below(i, n):
    return (2 * n - 2 - i) // n


def _step_ok(i, d, n):
    if d < 0:
        return _above(i, n)
    if d > 0:
        return _below(i, n)
    return 1


def coarse_kernel(n_sub, n_grp, block_ref, idx_ref, out_ref, buf, send_sem, recv_sem):
    s = lax.axis_index("sub")
    g = lax.axis_index("grp")
    rows = block_ref.shape[0]
    barrier = pltpu.get_barrier_semaphore()

    def peers():
        for ds in (-1, 0, 1):
            for gt in range(n_grp):
                yield ds, gt

    def exists(ds, gt):
        if ds < 0:
            return s + ds >= 0
        if ds > 0:
            return s + ds < n_sub
        return g != gt

    for ds, gt in peers():
        def signal(ds=ds, gt=gt):
            pl.semaphore_signal(barrier, inc=1, device_id=(s + ds, gt), device_id_type=MESH)
        pl.when(exists(ds, gt))(signal)
    count = (n_grp - 1) + n_grp * (_above(s, n_sub) + _below(s, n_sub))
    pl.semaphore_wait(barrier, count)

    copies = []
    for ds, gt in peers():
        slot_there = (1 - ds) * n_grp + g
        copy = pltpu.make_async_remote_copy(
            src_ref=block_ref,
            dst_ref=buf.at[pl.ds(slot_there * rows, rows)],
            send_sem=send_sem.at[(ds + 1) * n_grp + gt],
            recv_sem=recv_sem.at[slot_there],
            device_id=(s + ds, gt),
            device_id_type=MESH,
        )
        pl.when(exists(ds, gt))(copy.start)
        copies.append(copy)
    buf[pl.ds((n_grp + g) * rows, rows), :] = block_ref[...]
    for (ds, gt), copy in zip(peers(), copies):
        pl.when(exists(ds, gt))(copy.wait_send)
    for dr in (-1, 0, 1):
        for gr in range(n_grp):
            slot_here = (dr + 1) * n_grp + gr
            recv = pltpu.make_async_remote_copy(
                src_ref=block_ref,
                dst_ref=buf.at[pl.ds(slot_here * rows, rows)],
                send_sem=send_sem.at[slot_here],
                recv_sem=recv_sem.at[slot_here],
                device_id=(s + dr, gr),
                device_id_type=MESH,
            )
            pl.when(exists(dr, gr))(recv.wait_recv)
    first = (s - 1) * n_grp * rows
    for r in range(idx_ref.shape[1]):
        row = jnp.minimum(jnp.maximum(idx_ref[0, r] - first, 0), buf.shape[0] - 1)
        out_ref[pl.ds(r, 1), :] = buf[pl.ds(row, 1), :]


def face_kernel(
    n_sub, n_grp, send_ref, stress_ref, own_ref, spread_ref, vol_ref, out_ref, buf, added, acc,
    send_sem, recv_sem,
):
    s = lax.axis_index("sub")
    g = lax.axis_index("grp")
    barrier = pltpu.get_barrier_semaphore()

    def exists(ds, dg):
        conds = []
        if ds < 0:
            conds.append(s + ds >= 0)
        if ds > 0:
            conds.append(s + ds < n_sub)
        if dg < 0:
            conds.append(g + dg >= 0)
        if dg > 0:
            conds.append(g + dg < n_grp)
        cond = conds[0]
        for c in conds[1:]:
            cond = jnp.logical_and(cond, c)
        return cond

    for ds, dg, _, _ in DIRECTIONS:
        def signal(ds=ds, dg=dg):
            pl.semaphore_signal(barrier, inc=1, device_id=(s + ds, g + dg), device_id_type=MESH)
        pl.when(exists(ds, dg))(signal)
    count = 0
    for ds, dg, _, _ in DIRECTIONS:
        count = count + _step_ok(s, ds, n_sub) * _step_ok(g, dg, n_grp)
    pl.semaphore_wait(barrier, count)

    copies = []
    for j, (k, lo, hi, row) in enumerate(SEND_PIECES):
        ds, dg = DIRECTIONS[k][:2]
        copy = pltpu.make_async_remote_copy(
            src_ref=send_ref.at[:, pl.ds(lo, hi - lo)],
            dst_ref=buf.at[:, pl.ds(row, hi - lo)],
            send_sem=send_sem.at[j],
            recv_sem=recv_sem.at[j],
            device_id=(s + ds, g + dg),
            device_id_type=MESH,
        )
        pl.when(exists(ds, dg))(copy.start)
        copies.append(copy)
    added[...] = jnp.zeros(added.shape, added.dtype)
    for c in range(acc.shape[0]):
        acc[c] = jnp.dot(
            own_ref[...], stress_ref[c], precision=lax.Precision.HIGHEST,
            preferred_element_type=jnp.float32,
        )
    for j, (k, lo, hi, row) in enumerate(SEND_PIECES):
        ds, dg = DIRECTIONS[k][:2]
        pl.when(exists(ds, dg))(copies[j].wait_send)
    for k, (ds, dg, _, _) in enumerate(DIRECTIONS):
        mine = [j for j, piece in enumerate(SEND_PIECES) if piece[0] == k]

        def take(k=k, mine=mine):
            for j in mine:
                copies[j].wait_recv()
            for lo, hi, row in RECV_PIECES[k]:
                added[:, lo:hi, :] += buf[:, row:row + hi - lo, :]

        pl.when(exists(-ds, -dg))(take)
    for c in range(acc.shape[0]):
        total = acc[c] + jnp.dot(
            spread_ref[...], added[c], precision=lax.Precision.HIGHEST,
            preferred_element_type=jnp.float32,
        )
        out_ref[c] = (total / vol_ref[...]).astype(out_ref.dtype)


def fetch_corners(block, corner_idx, n_sub, n_grp):
    rows, width = block.shape
    slots = 3 * n_grp
    return pl.pallas_call(
        functools.partial(coarse_kernel, n_sub, n_grp),
        out_shape=jax.ShapeDtypeStruct((corner_idx.shape[1], width), block.dtype),
        in_specs=[
            pl.BlockSpec(memory_space=pltpu.VMEM),
            pl.BlockSpec(memory_space=pltpu.SMEM),
        ],
        out_specs=pl.BlockSpec(memory_space=pltpu.VMEM),
        scratch_shapes=[
            pltpu.VMEM((slots * rows, width), block.dtype),
            pltpu.SemaphoreType.DMA((slots,)),
            pltpu.SemaphoreType.DMA((slots,)),
        ],
        compiler_params=pltpu.CompilerParams(collective_id=0, has_side_effects=True),
    )(block, corner_idx)


def exchange_faces(send, stress, own, spread, volume, n_sub, n_grp):
    parts, nodes = stress.shape[0], own.shape[0]
    return pl.pallas_call(
        functools.partial(face_kernel, n_sub, n_grp),
        out_shape=jax.ShapeDtypeStruct((parts, nodes, send.shape[2]), jnp.bfloat16),
        in_specs=[pl.BlockSpec(memory_space=pltpu.VMEM)] * 5,
        out_specs=pl.BlockSpec(memory_space=pltpu.VMEM),
        scratch_shapes=[
            pltpu.VMEM((send.shape[0], int(SLOT_START[-1]), send.shape[2]), send.dtype),
            pltpu.VMEM(send.shape, send.dtype),
            pltpu.VMEM((parts, nodes, send.shape[2]), jnp.float32),
            pltpu.SemaphoreType.DMA((len(SEND_PIECES),)),
            pltpu.SemaphoreType.DMA((len(SEND_PIECES),)),
        ],
        compiler_params=pltpu.CompilerParams(collective_id=1, has_side_effects=True),
    )(send, stress, own, spread, volume)


def shards(
    n_sub,
    n_grp,
    coarse,
    corner_idx,
    coupling,
    force,
    panel_inv,
    panel_nodes,
    strain_disp,
    modulus,
    connect,
    interface,
    nodal_volume,
):
    corner_vals = fetch_corners(coarse, corner_idx, n_sub, n_grp)
    node_count = force.shape[0]
    load_cases = force.shape[2]
    panels = panel_inv.shape[0]
    panel_rows = panel_inv.shape[1]
    correction = jnp.dot(coupling.astype(jnp.float32), corner_vals, precision=lax.Precision.HIGHEST)
    live_mask = jnp.arange(panel_rows)[None, :] < 3 * panel_nodes[0][:, None]
    reduced = (force.reshape(3 * node_count, load_cases).astype(jnp.float32) - correction).reshape(
        panels, panel_rows, load_cases
    )
    reduced = jnp.where(live_mask[:, :, None], reduced, 0.0).astype(jnp.bfloat16)
    solved = jnp.einsum("prc,pcl->prl", panel_inv, reduced, preferred_element_type=jnp.float32)
    displaced = jnp.where(live_mask[:, :, None], solved, 0.0).astype(jnp.bfloat16)
    by_component = (
        displaced.reshape(panels, panel_rows // 3, 3, load_cases)
        .transpose(2, 0, 1, 3)
        .reshape(3, node_count, load_cases)
    )
    elem_count = connect.shape[1]
    node_range = jnp.arange(node_count, dtype=jnp.int32)
    corner_of = (connect.T.reshape(-1)[:, None] == node_range[None, :]).astype(jnp.bfloat16)
    element = jnp.einsum("xn,cnl->xcl", corner_of, by_component, preferred_element_type=jnp.float32)
    element = element.astype(jnp.bfloat16).reshape(elem_count, 24, load_cases)
    strain = jnp.einsum("ije,ejl->eil", strain_disp, element, preferred_element_type=jnp.float32)
    stress = (
        jnp.einsum("ik,ekl->iel", iso_matrix(), strain, precision=lax.Precision.HIGHEST)
        * modulus[None, :, None]
    )
    incidence = jnp.sum(
        (connect[:, None, :] == node_range[None, :, None]).astype(jnp.float32), axis=0
    )
    picker = (interface[0][:, None] == node_range[None, :]).astype(jnp.float32)
    send = jnp.einsum(
        "re,cel->crl", jnp.dot(picker, incidence), stress, precision=lax.Precision.HIGHEST
    )
    spread = (node_range[:, None] == interface[0][None, :]).astype(jnp.float32)
    volume = nodal_volume.reshape(node_count, 1)
    stress_out = exchange_faces(send, stress, incidence, spread, volume, n_sub, n_grp).transpose(1, 0, 2)
    return (by_component.transpose(1, 0, 2), stress_out)


def solution(mesh):
    n_sub = mesh.shape["sub"]
    n_grp = mesh.shape["grp"]
    placed = (
        P(("sub", "grp"), None),
        P(("sub", "grp"), None),
        P(("sub", "grp"), None),
        P(("sub", "grp"), None, None),
        P(("sub", "grp"), None, None),
        P(("sub", "grp"), None),
        P(None, None, ("sub", "grp")),
        P(("sub", "grp")),
        P(None, ("sub", "grp")),
        P(("sub", "grp"), None),
        P(("sub", "grp")),
    )
    return jax.shard_map(
        functools.partial(shards, n_sub, n_grp),
        mesh=mesh,
        in_specs=placed,
        out_specs=(P(("sub", "grp"), None, None), P(("sub", "grp"), None, None)),
        check_vma=False,
    )
```

```python
import functools

import jax
import jax.numpy as jnp
import numpy as np
from jax import lax
from jax.experimental import pallas as pl
from jax.experimental.pallas import tpu as pltpu
from jax.sharding import PartitionSpec as P

NIS = 64
NIG = 32
NED = 8

MESH = pl.DeviceIdType.MESH

POISSON = 0.3

SUB_LO = np.arange(0, NIS)
SUB_HI = np.arange(NIS, 2 * NIS)
GRP_LO = np.arange(2 * NIS, 2 * NIS + NIG)
GRP_HI = np.arange(2 * NIS + NIG, 2 * NIS + 2 * NIG)
_E0 = 2 * NIS + 2 * NIG
EDGE_LL = np.arange(_E0, _E0 + NED)
EDGE_LH = np.arange(_E0 + NED, _E0 + 2 * NED)
EDGE_HL = np.arange(_E0 + 2 * NED, _E0 + 3 * NED)
EDGE_HH = np.arange(_E0 + 3 * NED, _E0 + 4 * NED)

DIRECTIONS = (
    (1, 0, (SUB_HI, EDGE_HL, EDGE_HH), (SUB_LO, EDGE_LL, EDGE_LH)),
    (-1, 0, (SUB_LO, EDGE_LL, EDGE_LH), (SUB_HI, EDGE_HL, EDGE_HH)),
    (0, 1, (GRP_HI, EDGE_LH, EDGE_HH), (GRP_LO, EDGE_LL, EDGE_HL)),
    (0, -1, (GRP_LO, EDGE_LL, EDGE_HL), (GRP_HI, EDGE_LH, EDGE_HH)),
    (1, 1, (EDGE_HH,), (EDGE_LL,)),
    (1, -1, (EDGE_HL,), (EDGE_LH,)),
    (-1, 1, (EDGE_LH,), (EDGE_HL,)),
    (-1, -1, (EDGE_LL,), (EDGE_HH,)),
)
SLOT_ROWS = [sum(len(x) for x in d[2]) for d in DIRECTIONS]
SLOT_START = np.concatenate([[0], np.cumsum(SLOT_ROWS)])


def _runs(entries):
    runs = []
    for i in entries:
        if runs and runs[-1][1] == i:
            runs[-1][1] = i + 1
        else:
            runs.append([i, i + 1])
    return [(int(a), int(b)) for a, b in runs]


def _pieces(k, which):
    out = []
    row = int(SLOT_START[k])
    for a, b in _runs(np.concatenate(DIRECTIONS[k][which])):
        out.append((a, b, row))
        row += b - a
    return out


SEND_PIECES = [(k, a, b, row) for k in range(len(DIRECTIONS)) for a, b, row in _pieces(k, 2)]
RECV_PIECES = [_pieces(k, 3) for k in range(len(DIRECTIONS))]


def iso_matrix():
    lame_first = POISSON / ((1.0 + POISSON) * (1.0 - 2.0 * POISSON))
    shear_mod = 0.5 / (1.0 + POISSON)
    elastic = np.zeros((6, 6), np.float32)
    elastic[:3, :3] = lame_first
    elastic[:3, :3] += np.eye(3, dtype=np.float32) * np.float32(2.0 * shear_mod)
    elastic[3:, 3:] = np.eye(3, dtype=np.float32) * np.float32(shear_mod)
    return elastic


def _above(i, n):
    return (i + n - 1) // n


def _below(i, n):
    return (2 * n - 2 - i) // n


def _step_ok(i, d, n):
    if d < 0:
        return _above(i, n)
    if d > 0:
        return _below(i, n)
    return 1


def coarse_kernel(n_sub, n_grp, block_ref, idx_ref, out_ref, buf, send_sem, recv_sem):
    s = lax.axis_index("sub")
    g = lax.axis_index("grp")
    rows = block_ref.shape[0]
    barrier = pltpu.get_barrier_semaphore()

    def peers():
        for ds in (-1, 0, 1):
            for gt in range(n_grp):
                yield ds, gt

    def exists(ds, gt):
        if ds < 0:
            return s + ds >= 0
        if ds > 0:
            return s + ds < n_sub
        return g != gt

    for ds, gt in peers():
        def signal(ds=ds, gt=gt):
            pl.semaphore_signal(barrier, inc=1, device_id=(s + ds, gt), device_id_type=MESH)
        pl.when(exists(ds, gt))(signal)
    count = (n_grp - 1) + n_grp * (_above(s, n_sub) + _below(s, n_sub))
    pl.semaphore_wait(barrier, count)

    copies = []
    for ds, gt in peers():
        slot_there = (1 - ds) * n_grp + g
        copy = pltpu.make_async_remote_copy(
            src_ref=block_ref,
            dst_ref=buf.at[pl.ds(slot_there * rows, rows)],
            send_sem=send_sem.at[(ds + 1) * n_grp + gt],
            recv_sem=recv_sem.at[slot_there],
            device_id=(s + ds, gt),
            device_id_type=MESH,
        )
        pl.when(exists(ds, gt))(copy.start)
        copies.append(copy)
    buf[pl.ds((n_grp + g) * rows, rows), :] = block_ref[...]
    for (ds, gt), copy in zip(peers(), copies):
        pl.when(exists(ds, gt))(copy.wait_send)
    for dr in (-1, 0, 1):
        for gr in range(n_grp):
            slot_here = (dr + 1) * n_grp + gr
            recv = pltpu.make_async_remote_copy(
                src_ref=block_ref,
                dst_ref=buf.at[pl.ds(slot_here * rows, rows)],
                send_sem=send_sem.at[slot_here],
                recv_sem=recv_sem.at[slot_here],
                device_id=(s + dr, gr),
                device_id_type=MESH,
            )
            pl.when(exists(dr, gr))(recv.wait_recv)
    first = (s - 1) * n_grp * rows
    for r in range(idx_ref.shape[1]):
        row = jnp.minimum(jnp.maximum(idx_ref[0, r] - first, 0), buf.shape[0] - 1)
        out_ref[pl.ds(r, 1), :] = buf[pl.ds(row, 1), :]


def face_kernel(
    n_sub, n_grp, send_ref, stress_ref, own_ref, spread_ref, vol_ref, out_ref, buf, added, acc,
    send_sem, recv_sem,
):
    s = lax.axis_index("sub")
    g = lax.axis_index("grp")
    barrier = pltpu.get_barrier_semaphore()

    def exists(ds, dg):
        conds = []
        if ds < 0:
            conds.append(s + ds >= 0)
        if ds > 0:
            conds.append(s + ds < n_sub)
        if dg < 0:
            conds.append(g + dg >= 0)
        if dg > 0:
            conds.append(g + dg < n_grp)
        cond = conds[0]
        for c in conds[1:]:
            cond = jnp.logical_and(cond, c)
        return cond

    for ds, dg, _, _ in DIRECTIONS:
        def signal(ds=ds, dg=dg):
            pl.semaphore_signal(barrier, inc=1, device_id=(s + ds, g + dg), device_id_type=MESH)
        pl.when(exists(ds, dg))(signal)
    count = 0
    for ds, dg, _, _ in DIRECTIONS:
        count = count + _step_ok(s, ds, n_sub) * _step_ok(g, dg, n_grp)
    pl.semaphore_wait(barrier, count)

    copies = []
    for j, (k, lo, hi, row) in enumerate(SEND_PIECES):
        ds, dg = DIRECTIONS[k][:2]
        copy = pltpu.make_async_remote_copy(
            src_ref=send_ref.at[:, pl.ds(lo, hi - lo)],
            dst_ref=buf.at[:, pl.ds(row, hi - lo)],
            send_sem=send_sem.at[j],
            recv_sem=recv_sem.at[j],
            device_id=(s + ds, g + dg),
            device_id_type=MESH,
        )
        pl.when(exists(ds, dg))(copy.start)
        copies.append(copy)
    added[...] = jnp.zeros(added.shape, added.dtype)
    for c in range(acc.shape[0]):
        acc[c] = jnp.dot(
            own_ref[...], stress_ref[c], precision=lax.Precision.HIGHEST,
            preferred_element_type=jnp.float32,
        )
    for j, (k, lo, hi, row) in enumerate(SEND_PIECES):
        ds, dg = DIRECTIONS[k][:2]
        pl.when(exists(ds, dg))(copies[j].wait_send)
    for k, (ds, dg, _, _) in enumerate(DIRECTIONS):
        mine = [j for j, piece in enumerate(SEND_PIECES) if piece[0] == k]

        def take(k=k, mine=mine):
            for j in mine:
                copies[j].wait_recv()
            for lo, hi, row in RECV_PIECES[k]:
                added[:, lo:hi, :] += buf[:, row:row + hi - lo, :]

        pl.when(exists(-ds, -dg))(take)
    for c in range(acc.shape[0]):
        total = acc[c] + jnp.dot(
            spread_ref[...], added[c], precision=lax.Precision.HIGHEST,
            preferred_element_type=jnp.float32,
        )
        out_ref[c] = (total / vol_ref[...]).astype(out_ref.dtype)


def fetch_corners(block, corner_idx, n_sub, n_grp):
    rows, width = block.shape
    slots = 3 * n_grp
    return pl.pallas_call(
        functools.partial(coarse_kernel, n_sub, n_grp),
        out_shape=jax.ShapeDtypeStruct((corner_idx.shape[1], width), block.dtype),
        in_specs=[
            pl.BlockSpec(memory_space=pltpu.VMEM),
            pl.BlockSpec(memory_space=pltpu.SMEM),
        ],
        out_specs=pl.BlockSpec(memory_space=pltpu.VMEM),
        scratch_shapes=[
            pltpu.VMEM((slots * rows, width), block.dtype),
            pltpu.SemaphoreType.DMA((slots,)),
            pltpu.SemaphoreType.DMA((slots,)),
        ],
        compiler_params=pltpu.CompilerParams(collective_id=0, has_side_effects=True),
    )(block, corner_idx)


def exchange_faces(send, stress, own, spread, volume, n_sub, n_grp):
    parts, nodes = stress.shape[0], own.shape[0]
    return pl.pallas_call(
        functools.partial(face_kernel, n_sub, n_grp),
        out_shape=jax.ShapeDtypeStruct((parts, nodes, send.shape[2]), jnp.float32),
        in_specs=[pl.BlockSpec(memory_space=pltpu.VMEM)] * 5,
        out_specs=pl.BlockSpec(memory_space=pltpu.VMEM),
        scratch_shapes=[
            pltpu.VMEM((send.shape[0], int(SLOT_START[-1]), send.shape[2]), send.dtype),
            pltpu.VMEM(send.shape, send.dtype),
            pltpu.VMEM((parts, nodes, send.shape[2]), jnp.float32),
            pltpu.SemaphoreType.DMA((len(SEND_PIECES),)),
            pltpu.SemaphoreType.DMA((len(SEND_PIECES),)),
        ],
        compiler_params=pltpu.CompilerParams(collective_id=1, has_side_effects=True),
    )(send, stress, own, spread, volume)


def cast_kernel(in_ref, out_ref):
    out_ref[...] = in_ref[...].astype(out_ref.dtype)


def to_bf16(values):
    return pl.pallas_call(
        cast_kernel,
        out_shape=jax.ShapeDtypeStruct(values.shape, jnp.bfloat16),
        in_specs=[pl.BlockSpec(memory_space=pltpu.VMEM)],
        out_specs=pl.BlockSpec(memory_space=pltpu.VMEM),
    )(values)


def shards(
    n_sub,
    n_grp,
    coarse,
    corner_idx,
    coupling,
    force,
    panel_inv,
    panel_nodes,
    strain_disp,
    modulus,
    connect,
    interface,
    nodal_volume,
):
    corner_vals = fetch_corners(coarse, corner_idx, n_sub, n_grp)
    node_count = force.shape[0]
    load_cases = force.shape[2]
    panels = panel_inv.shape[0]
    panel_rows = panel_inv.shape[1]
    correction = jnp.dot(coupling.astype(jnp.float32), corner_vals, precision=lax.Precision.HIGHEST)
    live_mask = jnp.arange(panel_rows)[None, :] < 3 * panel_nodes[0][:, None]
    reduced = (force.reshape(3 * node_count, load_cases).astype(jnp.float32) - correction).reshape(
        panels, panel_rows, load_cases
    )
    reduced = jnp.where(live_mask[:, :, None], reduced, 0.0).astype(jnp.bfloat16)
    solved = jnp.einsum("prc,pcl->prl", panel_inv, reduced, preferred_element_type=jnp.float32)
    displaced = jnp.where(live_mask[:, :, None], solved, 0.0).astype(jnp.bfloat16)
    by_component = (
        displaced.reshape(panels, panel_rows // 3, 3, load_cases)
        .transpose(2, 0, 1, 3)
        .reshape(3, node_count, load_cases)
    )
    elem_count = connect.shape[1]
    node_range = jnp.arange(node_count, dtype=jnp.int32)
    corner_of = (connect.T.reshape(-1)[:, None] == node_range[None, :]).astype(jnp.bfloat16)
    element = jnp.einsum("xn,cnl->xcl", corner_of, by_component, preferred_element_type=jnp.float32)
    element = element.astype(jnp.bfloat16).reshape(elem_count, 24, load_cases)
    strain = jnp.einsum("ije,ejl->eil", strain_disp, element, preferred_element_type=jnp.float32)
    stress = (
        jnp.einsum("ik,ekl->iel", iso_matrix(), strain, precision=lax.Precision.HIGHEST)
        * modulus[None, :, None]
    )
    incidence = jnp.sum(
        (connect[:, None, :] == node_range[None, :, None]).astype(jnp.float32), axis=0
    )
    picker = (interface[0][:, None] == node_range[None, :]).astype(jnp.float32)
    send = jnp.einsum(
        "re,cel->crl", jnp.dot(picker, incidence), stress, precision=lax.Precision.HIGHEST
    )
    spread = (node_range[:, None] == interface[0][None, :]).astype(jnp.float32)
    volume = nodal_volume.reshape(node_count, 1)
    stress_out = to_bf16(exchange_faces(send, stress, incidence, spread, volume, n_sub, n_grp)).transpose(1, 0, 2)
    return (by_component.transpose(1, 0, 2), stress_out)


def solution(mesh):
    n_sub = mesh.shape["sub"]
    n_grp = mesh.shape["grp"]
    placed = (
        P(("sub", "grp"), None),
        P(("sub", "grp"), None),
        P(("sub", "grp"), None),
        P(("sub", "grp"), None, None),
        P(("sub", "grp"), None, None),
        P(("sub", "grp"), None),
        P(None, None, ("sub", "grp")),
        P(("sub", "grp")),
        P(None, ("sub", "grp")),
        P(("sub", "grp"), None),
        P(("sub", "grp")),
    )
    return jax.shard_map(
        functools.partial(shards, n_sub, n_grp),
        mesh=mesh,
        in_specs=placed,
        out_specs=(P(("sub", "grp"), None, None), P(("sub", "grp"), None, None)),
        check_vma=False,
    )
```

```python
import functools

import jax
import jax.numpy as jnp
import numpy as np
from jax import lax
from jax.experimental import pallas as pl
from jax.experimental.pallas import tpu as pltpu
from jax.sharding import PartitionSpec as P

NIS = 64
NIG = 32
NED = 8

MESH = pl.DeviceIdType.MESH

POISSON = 0.3

SUB_LO = np.arange(0, NIS)
SUB_HI = np.arange(NIS, 2 * NIS)
GRP_LO = np.arange(2 * NIS, 2 * NIS + NIG)
GRP_HI = np.arange(2 * NIS + NIG, 2 * NIS + 2 * NIG)
_E0 = 2 * NIS + 2 * NIG
EDGE_LL = np.arange(_E0, _E0 + NED)
EDGE_LH = np.arange(_E0 + NED, _E0 + 2 * NED)
EDGE_HL = np.arange(_E0 + 2 * NED, _E0 + 3 * NED)
EDGE_HH = np.arange(_E0 + 3 * NED, _E0 + 4 * NED)

DIRECTIONS = (
    (1, 0, (SUB_HI, EDGE_HL, EDGE_HH), (SUB_LO, EDGE_LL, EDGE_LH)),
    (-1, 0, (SUB_LO, EDGE_LL, EDGE_LH), (SUB_HI, EDGE_HL, EDGE_HH)),
    (0, 1, (GRP_HI, EDGE_LH, EDGE_HH), (GRP_LO, EDGE_LL, EDGE_HL)),
    (0, -1, (GRP_LO, EDGE_LL, EDGE_HL), (GRP_HI, EDGE_LH, EDGE_HH)),
    (1, 1, (EDGE_HH,), (EDGE_LL,)),
    (1, -1, (EDGE_HL,), (EDGE_LH,)),
    (-1, 1, (EDGE_LH,), (EDGE_HL,)),
    (-1, -1, (EDGE_LL,), (EDGE_HH,)),
)
SLOT_ROWS = [sum(len(x) for x in d[2]) for d in DIRECTIONS]
SLOT_START = np.concatenate([[0], np.cumsum(SLOT_ROWS)])


def _runs(entries):
    runs = []
    for i in entries:
        if runs and runs[-1][1] == i:
            runs[-1][1] = i + 1
        else:
            runs.append([i, i + 1])
    return [(int(a), int(b)) for a, b in runs]


def _pieces(k, which):
    out = []
    row = int(SLOT_START[k])
    for a, b in _runs(np.concatenate(DIRECTIONS[k][which])):
        out.append((a, b, row))
        row += b - a
    return out


SEND_PIECES = [(k, a, b, row) for k in range(len(DIRECTIONS)) for a, b, row in _pieces(k, 2)]
RECV_PIECES = [_pieces(k, 3) for k in range(len(DIRECTIONS))]


def iso_matrix():
    lame_first = POISSON / ((1.0 + POISSON) * (1.0 - 2.0 * POISSON))
    shear_mod = 0.5 / (1.0 + POISSON)
    elastic = np.zeros((6, 6), np.float32)
    elastic[:3, :3] = lame_first
    elastic[:3, :3] += np.eye(3, dtype=np.float32) * np.float32(2.0 * shear_mod)
    elastic[3:, 3:] = np.eye(3, dtype=np.float32) * np.float32(shear_mod)
    return elastic


def _above(i, n):
    return (i + n - 1) // n


def _below(i, n):
    return (2 * n - 2 - i) // n


def _step_ok(i, d, n):
    if d < 0:
        return _above(i, n)
    if d > 0:
        return _below(i, n)
    return 1


def coarse_kernel(n_sub, n_grp, block_ref, idx_ref, out_ref, buf, send_sem, recv_sem):
    s = lax.axis_index("sub")
    g = lax.axis_index("grp")
    rows = block_ref.shape[0]
    barrier = pltpu.get_barrier_semaphore()

    def peers():
        for ds in (-1, 0, 1):
            for gt in range(n_grp):
                yield ds, gt

    def exists(ds, gt):
        if ds < 0:
            return s + ds >= 0
        if ds > 0:
            return s + ds < n_sub
        return g != gt

    for ds, gt in peers():
        def signal(ds=ds, gt=gt):
            pl.semaphore_signal(barrier, inc=1, device_id=(s + ds, gt), device_id_type=MESH)
        pl.when(exists(ds, gt))(signal)
    count = (n_grp - 1) + n_grp * (_above(s, n_sub) + _below(s, n_sub))
    pl.semaphore_wait(barrier, count)

    copies = []
    for ds, gt in peers():
        slot_there = (1 - ds) * n_grp + g
        copy = pltpu.make_async_remote_copy(
            src_ref=block_ref,
            dst_ref=buf.at[pl.ds(slot_there * rows, rows)],
            send_sem=send_sem.at[(ds + 1) * n_grp + gt],
            recv_sem=recv_sem.at[slot_there],
            device_id=(s + ds, gt),
            device_id_type=MESH,
        )
        pl.when(exists(ds, gt))(copy.start)
        copies.append(copy)
    buf[pl.ds((n_grp + g) * rows, rows), :] = block_ref[...]
    for (ds, gt), copy in zip(peers(), copies):
        pl.when(exists(ds, gt))(copy.wait_send)
    for dr in (-1, 0, 1):
        for gr in range(n_grp):
            slot_here = (dr + 1) * n_grp + gr
            recv = pltpu.make_async_remote_copy(
                src_ref=block_ref,
                dst_ref=buf.at[pl.ds(slot_here * rows, rows)],
                send_sem=send_sem.at[slot_here],
                recv_sem=recv_sem.at[slot_here],
                device_id=(s + dr, gr),
                device_id_type=MESH,
            )
            pl.when(exists(dr, gr))(recv.wait_recv)
    first = (s - 1) * n_grp * rows
    for r in range(idx_ref.shape[1]):
        row = jnp.minimum(jnp.maximum(idx_ref[0, r] - first, 0), buf.shape[0] - 1)
        out_ref[pl.ds(r, 1), :] = buf[pl.ds(row, 1), :]


def face_kernel(
    n_sub, n_grp, send_ref, stress_ref, own_ref, spread_ref, out_ref, buf, added, acc, send_sem, recv_sem
):
    s = lax.axis_index("sub")
    g = lax.axis_index("grp")
    barrier = pltpu.get_barrier_semaphore()

    def exists(ds, dg):
        conds = []
        if ds < 0:
            conds.append(s + ds >= 0)
        if ds > 0:
            conds.append(s + ds < n_sub)
        if dg < 0:
            conds.append(g + dg >= 0)
        if dg > 0:
            conds.append(g + dg < n_grp)
        cond = conds[0]
        for c in conds[1:]:
            cond = jnp.logical_and(cond, c)
        return cond

    for ds, dg, _, _ in DIRECTIONS:
        def signal(ds=ds, dg=dg):
            pl.semaphore_signal(barrier, inc=1, device_id=(s + ds, g + dg), device_id_type=MESH)
        pl.when(exists(ds, dg))(signal)
    count = 0
    for ds, dg, _, _ in DIRECTIONS:
        count = count + _step_ok(s, ds, n_sub) * _step_ok(g, dg, n_grp)
    pl.semaphore_wait(barrier, count)

    copies = []
    for j, (k, lo, hi, row) in enumerate(SEND_PIECES):
        ds, dg = DIRECTIONS[k][:2]
        copy = pltpu.make_async_remote_copy(
            src_ref=send_ref.at[:, pl.ds(lo, hi - lo)],
            dst_ref=buf.at[:, pl.ds(row, hi - lo)],
            send_sem=send_sem.at[j],
            recv_sem=recv_sem.at[j],
            device_id=(s + ds, g + dg),
            device_id_type=MESH,
        )
        pl.when(exists(ds, dg))(copy.start)
        copies.append(copy)
    added[...] = jnp.zeros(added.shape, added.dtype)
    for c in range(acc.shape[0]):
        acc[c] = jnp.dot(
            own_ref[...], stress_ref[c], precision=lax.Precision.HIGHEST,
            preferred_element_type=jnp.float32,
        )
    for j, (k, lo, hi, row) in enumerate(SEND_PIECES):
        ds, dg = DIRECTIONS[k][:2]
        pl.when(exists(ds, dg))(copies[j].wait_send)
    for k, (ds, dg, _, _) in enumerate(DIRECTIONS):
        mine = [j for j, piece in enumerate(SEND_PIECES) if piece[0] == k]

        def take(k=k, mine=mine):
            for j in mine:
                copies[j].wait_recv()
            for lo, hi, row in RECV_PIECES[k]:
                added[:, lo:hi, :] += buf[:, row:row + hi - lo, :]

        pl.when(exists(-ds, -dg))(take)
    for c in range(acc.shape[0]):
        total = acc[c] + jnp.dot(
            spread_ref[...], added[c], precision=lax.Precision.HIGHEST,
            preferred_element_type=jnp.float32,
        )
        out_ref[c] = total.astype(out_ref.dtype)


def fetch_corners(block, corner_idx, n_sub, n_grp):
    rows, width = block.shape
    slots = 3 * n_grp
    return pl.pallas_call(
        functools.partial(coarse_kernel, n_sub, n_grp),
        out_shape=jax.ShapeDtypeStruct((corner_idx.shape[1], width), block.dtype),
        in_specs=[
            pl.BlockSpec(memory_space=pltpu.VMEM),
            pl.BlockSpec(memory_space=pltpu.SMEM),
        ],
        out_specs=pl.BlockSpec(memory_space=pltpu.VMEM),
        scratch_shapes=[
            pltpu.VMEM((slots * rows, width), block.dtype),
            pltpu.SemaphoreType.DMA((slots,)),
            pltpu.SemaphoreType.DMA((slots,)),
        ],
        compiler_params=pltpu.CompilerParams(collective_id=0, has_side_effects=True),
    )(block, corner_idx)


def exchange_faces(send, stress, own, spread, n_sub, n_grp):
    parts, nodes = stress.shape[0], own.shape[0]
    return pl.pallas_call(
        functools.partial(face_kernel, n_sub, n_grp),
        out_shape=jax.ShapeDtypeStruct((parts, nodes, send.shape[2]), jnp.bfloat16),
        in_specs=[pl.BlockSpec(memory_space=pltpu.VMEM)] * 4,
        out_specs=pl.BlockSpec(memory_space=pltpu.VMEM),
        scratch_shapes=[
            pltpu.VMEM((send.shape[0], int(SLOT_START[-1]), send.shape[2]), send.dtype),
            pltpu.VMEM(send.shape, send.dtype),
            pltpu.VMEM((parts, nodes, send.shape[2]), jnp.float32),
            pltpu.SemaphoreType.DMA((len(SEND_PIECES),)),
            pltpu.SemaphoreType.DMA((len(SEND_PIECES),)),
        ],
        compiler_params=pltpu.CompilerParams(collective_id=1, has_side_effects=True),
    )(send, stress, own, spread)


def shards(
    n_sub,
    n_grp,
    coarse,
    corner_idx,
    coupling,
    force,
    panel_inv,
    panel_nodes,
    strain_disp,
    modulus,
    connect,
    interface,
    nodal_volume,
):
    corner_vals = fetch_corners(coarse, corner_idx, n_sub, n_grp)
    node_count = force.shape[0]
    load_cases = force.shape[2]
    panels = panel_inv.shape[0]
    panel_rows = panel_inv.shape[1]
    correction = jnp.dot(coupling.astype(jnp.float32), corner_vals, precision=lax.Precision.HIGH)
    live_mask = jnp.arange(panel_rows)[None, :] < 3 * panel_nodes[0][:, None]
    reduced = (force.reshape(3 * node_count, load_cases).astype(jnp.float32) - correction).reshape(
        panels, panel_rows, load_cases
    )
    reduced = jnp.where(live_mask[:, :, None], reduced, 0.0).astype(jnp.bfloat16)
    solved = jnp.einsum("prc,pcl->prl", panel_inv, reduced, preferred_element_type=jnp.float32)
    displaced = jnp.where(live_mask[:, :, None], solved, 0.0).astype(jnp.bfloat16)
    by_component = (
        displaced.reshape(panels, panel_rows // 3, 3, load_cases)
        .transpose(2, 0, 1, 3)
        .reshape(3, node_count, load_cases)
    )
    elem_count = connect.shape[1]
    node_range = jnp.arange(node_count, dtype=jnp.int32)
    corner_of = (connect.T.reshape(-1)[:, None] == node_range[None, :]).astype(jnp.bfloat16)
    element = jnp.einsum("xn,cnl->xcl", corner_of, by_component, preferred_element_type=jnp.float32)
    element = element.astype(jnp.bfloat16).reshape(elem_count, 24, load_cases)
    strain = jnp.einsum("ije,ejl->eil", strain_disp, element, preferred_element_type=jnp.float32)
    stress = (
        jnp.einsum("ik,ekl->iel", iso_matrix(), strain, precision=lax.Precision.HIGHEST)
        * modulus[None, :, None]
    )
    incidence = jnp.sum(
        (connect[:, None, :] == node_range[None, :, None]).astype(jnp.float32), axis=0
    )
    picker = (interface[0][:, None] == node_range[None, :]).astype(jnp.float32)
    send = jnp.einsum(
        "re,cel->crl", jnp.dot(picker, incidence), stress, precision=lax.Precision.HIGH
    )
    inverse_volume = 1.0 / nodal_volume
    own = incidence * inverse_volume[:, None]
    spread = picker.T * inverse_volume[:, None]
    stress_out = exchange_faces(send, stress, own, spread, n_sub, n_grp).transpose(1, 0, 2)
    return (by_component.transpose(1, 0, 2), stress_out)


def solution(mesh):
    n_sub = mesh.shape["sub"]
    n_grp = mesh.shape["grp"]
    placed = (
        P(("sub", "grp"), None),
        P(("sub", "grp"), None),
        P(("sub", "grp"), None),
        P(("sub", "grp"), None, None),
        P(("sub", "grp"), None, None),
        P(("sub", "grp"), None),
        P(None, None, ("sub", "grp")),
        P(("sub", "grp")),
        P(None, ("sub", "grp")),
        P(("sub", "grp"), None),
        P(("sub", "grp")),
    )
    return jax.shard_map(
        functools.partial(shards, n_sub, n_grp),
        mesh=mesh,
        in_specs=placed,
        out_specs=(P(("sub", "grp"), None, None), P(("sub", "grp"), None, None)),
        check_vma=False,
    )
```

```python
import functools

import jax
import jax.numpy as jnp
import numpy as np
from jax import lax
from jax.experimental import pallas as pl
from jax.experimental.pallas import tpu as pltpu
from jax.sharding import PartitionSpec as P

NIS = 64
NIG = 32
NED = 8

MESH = pl.DeviceIdType.MESH

POISSON = 0.3

SUB_LO = np.arange(0, NIS)
SUB_HI = np.arange(NIS, 2 * NIS)
GRP_LO = np.arange(2 * NIS, 2 * NIS + NIG)
GRP_HI = np.arange(2 * NIS + NIG, 2 * NIS + 2 * NIG)
_E0 = 2 * NIS + 2 * NIG
EDGE_LL = np.arange(_E0, _E0 + NED)
EDGE_LH = np.arange(_E0 + NED, _E0 + 2 * NED)
EDGE_HL = np.arange(_E0 + 2 * NED, _E0 + 3 * NED)
EDGE_HH = np.arange(_E0 + 3 * NED, _E0 + 4 * NED)

DIRECTIONS = (
    (1, 0, (SUB_HI, EDGE_HL, EDGE_HH), (SUB_LO, EDGE_LL, EDGE_LH)),
    (-1, 0, (SUB_LO, EDGE_LL, EDGE_LH), (SUB_HI, EDGE_HL, EDGE_HH)),
    (0, 1, (GRP_HI, EDGE_LH, EDGE_HH), (GRP_LO, EDGE_LL, EDGE_HL)),
    (0, -1, (GRP_LO, EDGE_LL, EDGE_HL), (GRP_HI, EDGE_LH, EDGE_HH)),
    (1, 1, (EDGE_HH,), (EDGE_LL,)),
    (1, -1, (EDGE_HL,), (EDGE_LH,)),
    (-1, 1, (EDGE_LH,), (EDGE_HL,)),
    (-1, -1, (EDGE_LL,), (EDGE_HH,)),
)
SLOT_ROWS = [sum(len(x) for x in d[2]) for d in DIRECTIONS]
SLOT_START = np.concatenate([[0], np.cumsum(SLOT_ROWS)])


def _runs(entries):
    runs = []
    for i in entries:
        if runs and runs[-1][1] == i:
            runs[-1][1] = i + 1
        else:
            runs.append([i, i + 1])
    return [(int(a), int(b)) for a, b in runs]


def _pieces(k, which):
    out = []
    row = int(SLOT_START[k])
    for a, b in _runs(np.concatenate(DIRECTIONS[k][which])):
        out.append((a, b, row))
        row += b - a
    return out


SEND_PIECES = [(k, a, b, row) for k in range(len(DIRECTIONS)) for a, b, row in _pieces(k, 2)]
RECV_PIECES = [_pieces(k, 3) for k in range(len(DIRECTIONS))]


def iso_matrix():
    lame_first = POISSON / ((1.0 + POISSON) * (1.0 - 2.0 * POISSON))
    shear_mod = 0.5 / (1.0 + POISSON)
    elastic = np.zeros((6, 6), np.float32)
    elastic[:3, :3] = lame_first
    elastic[:3, :3] += np.eye(3, dtype=np.float32) * np.float32(2.0 * shear_mod)
    elastic[3:, 3:] = np.eye(3, dtype=np.float32) * np.float32(shear_mod)
    return elastic


def _above(i, n):
    return (i + n - 1) // n


def _below(i, n):
    return (2 * n - 2 - i) // n


def _step_ok(i, d, n):
    if d < 0:
        return _above(i, n)
    if d > 0:
        return _below(i, n)
    return 1


def coarse_kernel(n_sub, n_grp, block_ref, idx_ref, out_ref, buf, send_sem, recv_sem):
    s = lax.axis_index("sub")
    g = lax.axis_index("grp")
    rows = block_ref.shape[0]
    barrier = pltpu.get_barrier_semaphore()

    def peers():
        for ds in (-1, 0, 1):
            for gt in range(n_grp):
                yield ds, gt

    def exists(ds, gt):
        if ds < 0:
            return s + ds >= 0
        if ds > 0:
            return s + ds < n_sub
        return g != gt

    for ds, gt in peers():
        def signal(ds=ds, gt=gt):
            pl.semaphore_signal(barrier, inc=1, device_id=(s + ds, gt), device_id_type=MESH)
        pl.when(exists(ds, gt))(signal)
    count = (n_grp - 1) + n_grp * (_above(s, n_sub) + _below(s, n_sub))
    pl.semaphore_wait(barrier, count)

    copies = []
    for ds, gt in peers():
        slot_there = (1 - ds) * n_grp + g
        copy = pltpu.make_async_remote_copy(
            src_ref=block_ref,
            dst_ref=buf.at[pl.ds(slot_there * rows, rows)],
            send_sem=send_sem.at[(ds + 1) * n_grp + gt],
            recv_sem=recv_sem.at[slot_there],
            device_id=(s + ds, gt),
            device_id_type=MESH,
        )
        pl.when(exists(ds, gt))(copy.start)
        copies.append(copy)
    buf[pl.ds((n_grp + g) * rows, rows), :] = block_ref[...]
    for (ds, gt), copy in zip(peers(), copies):
        pl.when(exists(ds, gt))(copy.wait_send)
    for dr in (-1, 0, 1):
        for gr in range(n_grp):
            slot_here = (dr + 1) * n_grp + gr
            recv = pltpu.make_async_remote_copy(
                src_ref=block_ref,
                dst_ref=buf.at[pl.ds(slot_here * rows, rows)],
                send_sem=send_sem.at[slot_here],
                recv_sem=recv_sem.at[slot_here],
                device_id=(s + dr, gr),
                device_id_type=MESH,
            )
            pl.when(exists(dr, gr))(recv.wait_recv)
    first = (s - 1) * n_grp * rows
    for r in range(idx_ref.shape[1]):
        row = jnp.minimum(jnp.maximum(idx_ref[0, r] - first, 0), buf.shape[0] - 1)
        out_ref[pl.ds(r, 1), :] = buf[pl.ds(row, 1), :]


def face_kernel(
    n_sub, n_grp, send_ref, stress_ref, own_ref, spread_ref, out_ref, buf, added, acc, send_sem, recv_sem
):
    s = lax.axis_index("sub")
    g = lax.axis_index("grp")
    barrier = pltpu.get_barrier_semaphore()

    def exists(ds, dg):
        conds = []
        if ds < 0:
            conds.append(s + ds >= 0)
        if ds > 0:
            conds.append(s + ds < n_sub)
        if dg < 0:
            conds.append(g + dg >= 0)
        if dg > 0:
            conds.append(g + dg < n_grp)
        cond = conds[0]
        for c in conds[1:]:
            cond = jnp.logical_and(cond, c)
        return cond

    for ds, dg, _, _ in DIRECTIONS:
        def signal(ds=ds, dg=dg):
            pl.semaphore_signal(barrier, inc=1, device_id=(s + ds, g + dg), device_id_type=MESH)
        pl.when(exists(ds, dg))(signal)
    count = 0
    for ds, dg, _, _ in DIRECTIONS:
        count = count + _step_ok(s, ds, n_sub) * _step_ok(g, dg, n_grp)
    pl.semaphore_wait(barrier, count)

    copies = []
    for j, (k, lo, hi, row) in enumerate(SEND_PIECES):
        ds, dg = DIRECTIONS[k][:2]
        copy = pltpu.make_async_remote_copy(
            src_ref=send_ref.at[:, pl.ds(lo, hi - lo)],
            dst_ref=buf.at[:, pl.ds(row, hi - lo)],
            send_sem=send_sem.at[j],
            recv_sem=recv_sem.at[j],
            device_id=(s + ds, g + dg),
            device_id_type=MESH,
        )
        pl.when(exists(ds, dg))(copy.start)
        copies.append(copy)
    added[...] = jnp.zeros(added.shape, added.dtype)
    for c in range(acc.shape[0]):
        acc[c] = jnp.dot(
            own_ref[...], stress_ref[c], precision=lax.Precision.HIGH,
            preferred_element_type=jnp.float32,
        )
    for j, (k, lo, hi, row) in enumerate(SEND_PIECES):
        ds, dg = DIRECTIONS[k][:2]
        pl.when(exists(ds, dg))(copies[j].wait_send)
    for k, (ds, dg, _, _) in enumerate(DIRECTIONS):
        mine = [j for j, piece in enumerate(SEND_PIECES) if piece[0] == k]

        def take(k=k, mine=mine):
            for j in mine:
                copies[j].wait_recv()
            for lo, hi, row in RECV_PIECES[k]:
                added[:, lo:hi, :] += buf[:, row:row + hi - lo, :]

        pl.when(exists(-ds, -dg))(take)
    for c in range(acc.shape[0]):
        total = acc[c] + jnp.dot(
            spread_ref[...], added[c], precision=lax.Precision.HIGH,
            preferred_element_type=jnp.float32,
        )
        out_ref[c] = total.astype(out_ref.dtype)


def fetch_corners(block, corner_idx, n_sub, n_grp):
    rows, width = block.shape
    slots = 3 * n_grp
    return pl.pallas_call(
        functools.partial(coarse_kernel, n_sub, n_grp),
        out_shape=jax.ShapeDtypeStruct((corner_idx.shape[1], width), block.dtype),
        in_specs=[
            pl.BlockSpec(memory_space=pltpu.VMEM),
            pl.BlockSpec(memory_space=pltpu.SMEM),
        ],
        out_specs=pl.BlockSpec(memory_space=pltpu.VMEM),
        scratch_shapes=[
            pltpu.VMEM((slots * rows, width), block.dtype),
            pltpu.SemaphoreType.DMA((slots,)),
            pltpu.SemaphoreType.DMA((slots,)),
        ],
        compiler_params=pltpu.CompilerParams(collective_id=0, has_side_effects=True),
    )(block, corner_idx)


def exchange_faces(send, stress, own, spread, n_sub, n_grp):
    parts, nodes = stress.shape[0], own.shape[0]
    return pl.pallas_call(
        functools.partial(face_kernel, n_sub, n_grp),
        out_shape=jax.ShapeDtypeStruct((parts, nodes, send.shape[2]), jnp.bfloat16),
        in_specs=[pl.BlockSpec(memory_space=pltpu.VMEM)] * 4,
        out_specs=pl.BlockSpec(memory_space=pltpu.VMEM),
        scratch_shapes=[
            pltpu.VMEM((send.shape[0], int(SLOT_START[-1]), send.shape[2]), send.dtype),
            pltpu.VMEM(send.shape, send.dtype),
            pltpu.VMEM((parts, nodes, send.shape[2]), jnp.float32),
            pltpu.SemaphoreType.DMA((len(SEND_PIECES),)),
            pltpu.SemaphoreType.DMA((len(SEND_PIECES),)),
        ],
        compiler_params=pltpu.CompilerParams(collective_id=1, has_side_effects=True),
    )(send, stress, own, spread)


def shards(
    n_sub,
    n_grp,
    coarse,
    corner_idx,
    coupling,
    force,
    panel_inv,
    panel_nodes,
    strain_disp,
    modulus,
    connect,
    interface,
    nodal_volume,
):
    corner_vals = fetch_corners(coarse, corner_idx, n_sub, n_grp)
    node_count = force.shape[0]
    load_cases = force.shape[2]
    panels = panel_inv.shape[0]
    panel_rows = panel_inv.shape[1]
    correction = jnp.dot(coupling.astype(jnp.float32), corner_vals, precision=lax.Precision.HIGH)
    live_mask = jnp.arange(panel_rows)[None, :] < 3 * panel_nodes[0][:, None]
    reduced = (force.reshape(3 * node_count, load_cases).astype(jnp.float32) - correction).reshape(
        panels, panel_rows, load_cases
    )
    reduced = jnp.where(live_mask[:, :, None], reduced, 0.0).astype(jnp.bfloat16)
    solved = jnp.einsum("prc,pcl->prl", panel_inv, reduced, preferred_element_type=jnp.float32)
    displaced = jnp.where(live_mask[:, :, None], solved, 0.0).astype(jnp.bfloat16)
    by_component = (
        displaced.reshape(panels, panel_rows // 3, 3, load_cases)
        .transpose(2, 0, 1, 3)
        .reshape(3, node_count, load_cases)
    )
    elem_count = connect.shape[1]
    node_range = jnp.arange(node_count, dtype=jnp.int32)
    corner_of = (connect.T.reshape(-1)[:, None] == node_range[None, :]).astype(jnp.bfloat16)
    element = jnp.einsum("xn,cnl->xcl", corner_of, by_component, preferred_element_type=jnp.float32)
    element = element.astype(jnp.bfloat16).reshape(elem_count, 24, load_cases)
    strain = jnp.einsum("ije,ejl->eil", strain_disp, element, preferred_element_type=jnp.float32)
    stress = (
        jnp.einsum("ik,ekl->iel", iso_matrix(), strain, precision=lax.Precision.HIGHEST)
        * modulus[None, :, None]
    )
    incidence = jnp.sum(
        (connect[:, None, :] == node_range[None, :, None]).astype(jnp.float32), axis=0
    )
    picker = (interface[0][:, None] == node_range[None, :]).astype(jnp.float32)
    send = jnp.einsum(
        "re,cel->crl", jnp.dot(picker, incidence), stress, precision=lax.Precision.HIGH
    )
    inverse_volume = 1.0 / nodal_volume
    own = incidence * inverse_volume[:, None]
    spread = picker.T * inverse_volume[:, None]
    stress_out = exchange_faces(send, stress, own, spread, n_sub, n_grp).transpose(1, 0, 2)
    return (by_component.transpose(1, 0, 2), stress_out)


def solution(mesh):
    n_sub = mesh.shape["sub"]
    n_grp = mesh.shape["grp"]
    placed = (
        P(("sub", "grp"), None),
        P(("sub", "grp"), None),
        P(("sub", "grp"), None),
        P(("sub", "grp"), None, None),
        P(("sub", "grp"), None, None),
        P(("sub", "grp"), None),
        P(None, None, ("sub", "grp")),
        P(("sub", "grp")),
        P(None, ("sub", "grp")),
        P(("sub", "grp"), None),
        P(("sub", "grp")),
    )
    return jax.shard_map(
        functools.partial(shards, n_sub, n_grp),
        mesh=mesh,
        in_specs=placed,
        out_specs=(P(("sub", "grp"), None, None), P(("sub", "grp"), None, None)),
        check_vma=False,
    )
```

```python
import functools

import jax
import jax.numpy as jnp
import numpy as np
from jax import lax
from jax.experimental import pallas as pl
from jax.experimental.pallas import tpu as pltpu
from jax.sharding import PartitionSpec as P

NIS = 64
NIG = 32
NED = 8

MESH = pl.DeviceIdType.MESH

POISSON = 0.3

SUB_LO = np.arange(0, NIS)
SUB_HI = np.arange(NIS, 2 * NIS)
GRP_LO = np.arange(2 * NIS, 2 * NIS + NIG)
GRP_HI = np.arange(2 * NIS + NIG, 2 * NIS + 2 * NIG)
_E0 = 2 * NIS + 2 * NIG
EDGE_LL = np.arange(_E0, _E0 + NED)
EDGE_LH = np.arange(_E0 + NED, _E0 + 2 * NED)
EDGE_HL = np.arange(_E0 + 2 * NED, _E0 + 3 * NED)
EDGE_HH = np.arange(_E0 + 3 * NED, _E0 + 4 * NED)

DIRECTIONS = (
    (1, 0, (SUB_HI, EDGE_HL, EDGE_HH), (SUB_LO, EDGE_LL, EDGE_LH)),
    (-1, 0, (SUB_LO, EDGE_LL, EDGE_LH), (SUB_HI, EDGE_HL, EDGE_HH)),
    (0, 1, (GRP_HI, EDGE_LH, EDGE_HH), (GRP_LO, EDGE_LL, EDGE_HL)),
    (0, -1, (GRP_LO, EDGE_LL, EDGE_HL), (GRP_HI, EDGE_LH, EDGE_HH)),
    (1, 1, (EDGE_HH,), (EDGE_LL,)),
    (1, -1, (EDGE_HL,), (EDGE_LH,)),
    (-1, 1, (EDGE_LH,), (EDGE_HL,)),
    (-1, -1, (EDGE_LL,), (EDGE_HH,)),
)
SLOT_ROWS = [sum(len(x) for x in d[2]) for d in DIRECTIONS]
SLOT_START = np.concatenate([[0], np.cumsum(SLOT_ROWS)])


def _runs(entries):
    runs = []
    for i in entries:
        if runs and runs[-1][1] == i:
            runs[-1][1] = i + 1
        else:
            runs.append([i, i + 1])
    return [(int(a), int(b)) for a, b in runs]


def _pieces(k, which):
    out = []
    row = int(SLOT_START[k])
    for a, b in _runs(np.concatenate(DIRECTIONS[k][which])):
        out.append((a, b, row))
        row += b - a
    return out


SEND_PIECES = [(k, a, b, row) for k in range(len(DIRECTIONS)) for a, b, row in _pieces(k, 2)]
RECV_PIECES = [_pieces(k, 3) for k in range(len(DIRECTIONS))]


def iso_matrix():
    lame_first = POISSON / ((1.0 + POISSON) * (1.0 - 2.0 * POISSON))
    shear_mod = 0.5 / (1.0 + POISSON)
    elastic = np.zeros((6, 6), np.float32)
    elastic[:3, :3] = lame_first
    elastic[:3, :3] += np.eye(3, dtype=np.float32) * np.float32(2.0 * shear_mod)
    elastic[3:, 3:] = np.eye(3, dtype=np.float32) * np.float32(shear_mod)
    return elastic


def _above(i, n):
    return (i + n - 1) // n


def _below(i, n):
    return (2 * n - 2 - i) // n


def _step_ok(i, d, n):
    if d < 0:
        return _above(i, n)
    if d > 0:
        return _below(i, n)
    return 1


def coarse_kernel(n_sub, n_grp, block_ref, idx_ref, out_ref, buf, send_sem, recv_sem):
    s = lax.axis_index("sub")
    g = lax.axis_index("grp")
    rows = block_ref.shape[0]
    barrier = pltpu.get_barrier_semaphore()

    def peers():
        for ds in (-1, 0, 1):
            for gt in range(n_grp):
                yield ds, gt

    def exists(ds, gt):
        if ds < 0:
            return s + ds >= 0
        if ds > 0:
            return s + ds < n_sub
        return g != gt

    for ds, gt in peers():
        def signal(ds=ds, gt=gt):
            pl.semaphore_signal(barrier, inc=1, device_id=(s + ds, gt), device_id_type=MESH)
        pl.when(exists(ds, gt))(signal)
    count = (n_grp - 1) + n_grp * (_above(s, n_sub) + _below(s, n_sub))
    pl.semaphore_wait(barrier, count)

    copies = []
    for ds, gt in peers():
        slot_there = (1 - ds) * n_grp + g
        copy = pltpu.make_async_remote_copy(
            src_ref=block_ref,
            dst_ref=buf.at[pl.ds(slot_there * rows, rows)],
            send_sem=send_sem.at[(ds + 1) * n_grp + gt],
            recv_sem=recv_sem.at[slot_there],
            device_id=(s + ds, gt),
            device_id_type=MESH,
        )
        pl.when(exists(ds, gt))(copy.start)
        copies.append(copy)
    buf[pl.ds((n_grp + g) * rows, rows), :] = block_ref[...]
    for (ds, gt), copy in zip(peers(), copies):
        pl.when(exists(ds, gt))(copy.wait_send)
    for dr in (-1, 0, 1):
        for gr in range(n_grp):
            slot_here = (dr + 1) * n_grp + gr
            recv = pltpu.make_async_remote_copy(
                src_ref=block_ref,
                dst_ref=buf.at[pl.ds(slot_here * rows, rows)],
                send_sem=send_sem.at[slot_here],
                recv_sem=recv_sem.at[slot_here],
                device_id=(s + dr, gr),
                device_id_type=MESH,
            )
            pl.when(exists(dr, gr))(recv.wait_recv)
    first = (s - 1) * n_grp * rows
    for r in range(idx_ref.shape[1]):
        row = jnp.minimum(jnp.maximum(idx_ref[0, r] - first, 0), buf.shape[0] - 1)
        out_ref[pl.ds(r, 1), :] = buf[pl.ds(row, 1), :]


def face_kernel(
    n_sub, n_grp, send_ref, stress_ref, own_ref, spread_ref, out_ref, buf, added, acc, send_sem, recv_sem
):
    s = lax.axis_index("sub")
    g = lax.axis_index("grp")
    barrier = pltpu.get_barrier_semaphore()

    def exists(ds, dg):
        conds = []
        if ds < 0:
            conds.append(s + ds >= 0)
        if ds > 0:
            conds.append(s + ds < n_sub)
        if dg < 0:
            conds.append(g + dg >= 0)
        if dg > 0:
            conds.append(g + dg < n_grp)
        cond = conds[0]
        for c in conds[1:]:
            cond = jnp.logical_and(cond, c)
        return cond

    for ds, dg, _, _ in DIRECTIONS:
        def signal(ds=ds, dg=dg):
            pl.semaphore_signal(barrier, inc=1, device_id=(s + ds, g + dg), device_id_type=MESH)
        pl.when(exists(ds, dg))(signal)
    count = 0
    for ds, dg, _, _ in DIRECTIONS:
        count = count + _step_ok(s, ds, n_sub) * _step_ok(g, dg, n_grp)
    pl.semaphore_wait(barrier, count)

    copies = []
    for j, (k, lo, hi, row) in enumerate(SEND_PIECES):
        ds, dg = DIRECTIONS[k][:2]
        copy = pltpu.make_async_remote_copy(
            src_ref=send_ref.at[:, pl.ds(lo, hi - lo)],
            dst_ref=buf.at[:, pl.ds(row, hi - lo)],
            send_sem=send_sem.at[j],
            recv_sem=recv_sem.at[j],
            device_id=(s + ds, g + dg),
            device_id_type=MESH,
        )
        pl.when(exists(ds, dg))(copy.start)
        copies.append(copy)
    added[...] = jnp.zeros(added.shape, added.dtype)
    for c in range(acc.shape[0]):
        acc[c] = jnp.dot(
            own_ref[...], stress_ref[c], precision=lax.Precision.HIGH,
            preferred_element_type=jnp.float32,
        )
    for j, (k, lo, hi, row) in enumerate(SEND_PIECES):
        ds, dg = DIRECTIONS[k][:2]
        pl.when(exists(ds, dg))(copies[j].wait_send)
    for k, (ds, dg, _, _) in enumerate(DIRECTIONS):
        mine = [j for j, piece in enumerate(SEND_PIECES) if piece[0] == k]

        def take(k=k, mine=mine):
            for j in mine:
                copies[j].wait_recv()
            for lo, hi, row in RECV_PIECES[k]:
                added[:, lo:hi, :] += buf[:, row:row + hi - lo, :]

        pl.when(exists(-ds, -dg))(take)
    for c in range(acc.shape[0]):
        total = acc[c] + jnp.dot(
            spread_ref[...], added[c], precision=lax.Precision.HIGH,
            preferred_element_type=jnp.float32,
        )
        out_ref[c] = total.astype(out_ref.dtype)


def fetch_corners(block, corner_idx, n_sub, n_grp):
    rows, width = block.shape
    slots = 3 * n_grp
    return pl.pallas_call(
        functools.partial(coarse_kernel, n_sub, n_grp),
        out_shape=jax.ShapeDtypeStruct((corner_idx.shape[1], width), block.dtype),
        in_specs=[
            pl.BlockSpec(memory_space=pltpu.VMEM),
            pl.BlockSpec(memory_space=pltpu.SMEM),
        ],
        out_specs=pl.BlockSpec(memory_space=pltpu.VMEM),
        scratch_shapes=[
            pltpu.VMEM((slots * rows, width), block.dtype),
            pltpu.SemaphoreType.DMA((slots,)),
            pltpu.SemaphoreType.DMA((slots,)),
        ],
        compiler_params=pltpu.CompilerParams(collective_id=0, has_side_effects=True),
    )(block, corner_idx)


def exchange_faces(send, stress, own, spread, n_sub, n_grp):
    parts, nodes = stress.shape[0], own.shape[0]
    return pl.pallas_call(
        functools.partial(face_kernel, n_sub, n_grp),
        out_shape=jax.ShapeDtypeStruct((parts, nodes, send.shape[2]), jnp.bfloat16),
        in_specs=[pl.BlockSpec(memory_space=pltpu.VMEM)] * 4,
        out_specs=pl.BlockSpec(memory_space=pltpu.VMEM),
        scratch_shapes=[
            pltpu.VMEM((send.shape[0], int(SLOT_START[-1]), send.shape[2]), send.dtype),
            pltpu.VMEM(send.shape, send.dtype),
            pltpu.VMEM((parts, nodes, send.shape[2]), jnp.float32),
            pltpu.SemaphoreType.DMA((len(SEND_PIECES),)),
            pltpu.SemaphoreType.DMA((len(SEND_PIECES),)),
        ],
        compiler_params=pltpu.CompilerParams(collective_id=1, has_side_effects=True),
    )(send, stress, own, spread)


def shards(
    n_sub,
    n_grp,
    coarse,
    corner_idx,
    coupling,
    force,
    panel_inv,
    panel_nodes,
    strain_disp,
    modulus,
    connect,
    interface,
    nodal_volume,
):
    corner_vals = fetch_corners(coarse, corner_idx, n_sub, n_grp)
    node_count = force.shape[0]
    load_cases = force.shape[2]
    panels = panel_inv.shape[0]
    panel_rows = panel_inv.shape[1]
    correction = jnp.dot(coupling.astype(jnp.float32), corner_vals, precision=lax.Precision.HIGH)
    live_mask = jnp.arange(panel_rows)[None, :] < 3 * panel_nodes[0][:, None]
    reduced = (force.reshape(3 * node_count, load_cases).astype(jnp.float32) - correction).reshape(
        panels, panel_rows, load_cases
    )
    reduced = jnp.where(live_mask[:, :, None], reduced, 0.0).astype(jnp.bfloat16)
    solved = jnp.einsum("prc,pcl->prl", panel_inv, reduced, preferred_element_type=jnp.float32)
    displaced = jnp.where(live_mask[:, :, None], solved, 0.0).astype(jnp.bfloat16)
    by_component = (
        displaced.reshape(panels, panel_rows // 3, 3, load_cases)
        .transpose(2, 0, 1, 3)
        .reshape(3, node_count, load_cases)
    )
    elem_count = connect.shape[1]
    node_range = jnp.arange(node_count, dtype=jnp.int32)
    corner_of = (connect.T.reshape(-1)[:, None] == node_range[None, :]).astype(jnp.bfloat16)
    element = jnp.einsum("xn,cnl->xcl", corner_of, by_component, preferred_element_type=jnp.float32)
    element = element.astype(jnp.bfloat16).reshape(elem_count, 24, load_cases)
    strain = jnp.einsum("ije,ejl->eil", strain_disp, element, preferred_element_type=jnp.float32)
    stress = (
        jnp.einsum("ik,ekl->iel", iso_matrix(), strain, precision=lax.Precision.HIGH)
        * modulus[None, :, None]
    )
    incidence = jnp.sum(
        (connect[:, None, :] == node_range[None, :, None]).astype(jnp.float32), axis=0
    )
    picker = (interface[0][:, None] == node_range[None, :]).astype(jnp.float32)
    send = jnp.einsum(
        "re,cel->crl", jnp.dot(picker, incidence), stress, precision=lax.Precision.HIGH
    )
    inverse_volume = 1.0 / nodal_volume
    own = incidence * inverse_volume[:, None]
    spread = picker.T * inverse_volume[:, None]
    stress_out = exchange_faces(send, stress, own, spread, n_sub, n_grp).transpose(1, 0, 2)
    return (by_component.transpose(1, 0, 2), stress_out)


def solution(mesh):
    n_sub = mesh.shape["sub"]
    n_grp = mesh.shape["grp"]
    placed = (
        P(("sub", "grp"), None),
        P(("sub", "grp"), None),
        P(("sub", "grp"), None),
        P(("sub", "grp"), None, None),
        P(("sub", "grp"), None, None),
        P(("sub", "grp"), None),
        P(None, None, ("sub", "grp")),
        P(("sub", "grp")),
        P(None, ("sub", "grp")),
        P(("sub", "grp"), None),
        P(("sub", "grp")),
    )
    return jax.shard_map(
        functools.partial(shards, n_sub, n_grp),
        mesh=mesh,
        in_specs=placed,
        out_specs=(P(("sub", "grp"), None, None), P(("sub", "grp"), None, None)),
        check_vma=False,
    )
```

```python
import functools

import jax
import jax.numpy as jnp
import numpy as np
from jax import lax
from jax.experimental import pallas as pl
from jax.experimental.pallas import tpu as pltpu
from jax.sharding import PartitionSpec as P

NIS = 64
NIG = 32
NED = 8

MESH = pl.DeviceIdType.MESH

POISSON = 0.3

SUB_LO = np.arange(0, NIS)
SUB_HI = np.arange(NIS, 2 * NIS)
GRP_LO = np.arange(2 * NIS, 2 * NIS + NIG)
GRP_HI = np.arange(2 * NIS + NIG, 2 * NIS + 2 * NIG)
_E0 = 2 * NIS + 2 * NIG
EDGE_LL = np.arange(_E0, _E0 + NED)
EDGE_LH = np.arange(_E0 + NED, _E0 + 2 * NED)
EDGE_HL = np.arange(_E0 + 2 * NED, _E0 + 3 * NED)
EDGE_HH = np.arange(_E0 + 3 * NED, _E0 + 4 * NED)

DIRECTIONS = (
    (1, 0, (SUB_HI, EDGE_HL, EDGE_HH), (SUB_LO, EDGE_LL, EDGE_LH)),
    (-1, 0, (SUB_LO, EDGE_LL, EDGE_LH), (SUB_HI, EDGE_HL, EDGE_HH)),
    (0, 1, (GRP_HI, EDGE_LH, EDGE_HH), (GRP_LO, EDGE_LL, EDGE_HL)),
    (0, -1, (GRP_LO, EDGE_LL, EDGE_HL), (GRP_HI, EDGE_LH, EDGE_HH)),
    (1, 1, (EDGE_HH,), (EDGE_LL,)),
    (1, -1, (EDGE_HL,), (EDGE_LH,)),
    (-1, 1, (EDGE_LH,), (EDGE_HL,)),
    (-1, -1, (EDGE_LL,), (EDGE_HH,)),
)
SLOT_ROWS = [sum(len(x) for x in d[2]) for d in DIRECTIONS]
SLOT_START = np.concatenate([[0], np.cumsum(SLOT_ROWS)])


def _runs(entries):
    runs = []
    for i in entries:
        if runs and runs[-1][1] == i:
            runs[-1][1] = i + 1
        else:
            runs.append([i, i + 1])
    return [(int(a), int(b)) for a, b in runs]


def _pieces(k, which):
    out = []
    row = int(SLOT_START[k])
    for a, b in _runs(np.concatenate(DIRECTIONS[k][which])):
        out.append((a, b, row))
        row += b - a
    return out


SEND_PIECES = [(k, a, b, row) for k in range(len(DIRECTIONS)) for a, b, row in _pieces(k, 2)]
RECV_PIECES = [_pieces(k, 3) for k in range(len(DIRECTIONS))]


def iso_matrix():
    lame_first = POISSON / ((1.0 + POISSON) * (1.0 - 2.0 * POISSON))
    shear_mod = 0.5 / (1.0 + POISSON)
    elastic = np.zeros((6, 6), np.float32)
    elastic[:3, :3] = lame_first
    elastic[:3, :3] += np.eye(3, dtype=np.float32) * np.float32(2.0 * shear_mod)
    elastic[3:, 3:] = np.eye(3, dtype=np.float32) * np.float32(shear_mod)
    return elastic


def _above(i, n):
    return (i + n - 1) // n


def _below(i, n):
    return (2 * n - 2 - i) // n


def _step_ok(i, d, n):
    if d < 0:
        return _above(i, n)
    if d > 0:
        return _below(i, n)
    return 1


def coarse_kernel(n_sub, n_grp, block_ref, idx_ref, out_ref, buf, send_sem, recv_sem):
    s = lax.axis_index("sub")
    g = lax.axis_index("grp")
    rows = block_ref.shape[0]
    barrier = pltpu.get_barrier_semaphore()

    def peers():
        for ds in (-1, 0, 1):
            for gt in range(n_grp):
                yield ds, gt

    def exists(ds, gt):
        if ds < 0:
            return s + ds >= 0
        if ds > 0:
            return s + ds < n_sub
        return g != gt

    for ds, gt in peers():
        def signal(ds=ds, gt=gt):
            pl.semaphore_signal(barrier, inc=1, device_id=(s + ds, gt), device_id_type=MESH)
        pl.when(exists(ds, gt))(signal)
    count = (n_grp - 1) + n_grp * (_above(s, n_sub) + _below(s, n_sub))
    pl.semaphore_wait(barrier, count)

    copies = []
    for ds, gt in peers():
        slot_there = (1 - ds) * n_grp + g
        copy = pltpu.make_async_remote_copy(
            src_ref=block_ref,
            dst_ref=buf.at[pl.ds(slot_there * rows, rows)],
            send_sem=send_sem.at[(ds + 1) * n_grp + gt],
            recv_sem=recv_sem.at[slot_there],
            device_id=(s + ds, gt),
            device_id_type=MESH,
        )
        pl.when(exists(ds, gt))(copy.start)
        copies.append(copy)
    buf[pl.ds((n_grp + g) * rows, rows), :] = block_ref[...]
    for (ds, gt), copy in zip(peers(), copies):
        pl.when(exists(ds, gt))(copy.wait_send)
    for dr in (-1, 0, 1):
        for gr in range(n_grp):
            slot_here = (dr + 1) * n_grp + gr
            recv = pltpu.make_async_remote_copy(
                src_ref=block_ref,
                dst_ref=buf.at[pl.ds(slot_here * rows, rows)],
                send_sem=send_sem.at[slot_here],
                recv_sem=recv_sem.at[slot_here],
                device_id=(s + dr, gr),
                device_id_type=MESH,
            )
            pl.when(exists(dr, gr))(recv.wait_recv)
    first = (s - 1) * n_grp * rows
    for r in range(idx_ref.shape[1]):
        row = jnp.minimum(jnp.maximum(idx_ref[0, r] - first, 0), buf.shape[0] - 1)
        out_ref[pl.ds(r, 1), :] = buf[pl.ds(row, 1), :]


def face_kernel(
    n_sub, n_grp, send_ref, stress_ref, scaled_ref, out_ref, buf, added, acc, send_sem, recv_sem
):
    width = stress_ref.shape[1]
    s = lax.axis_index("sub")
    g = lax.axis_index("grp")
    barrier = pltpu.get_barrier_semaphore()

    def exists(ds, dg):
        conds = []
        if ds < 0:
            conds.append(s + ds >= 0)
        if ds > 0:
            conds.append(s + ds < n_sub)
        if dg < 0:
            conds.append(g + dg >= 0)
        if dg > 0:
            conds.append(g + dg < n_grp)
        cond = conds[0]
        for c in conds[1:]:
            cond = jnp.logical_and(cond, c)
        return cond

    for ds, dg, _, _ in DIRECTIONS:
        def signal(ds=ds, dg=dg):
            pl.semaphore_signal(barrier, inc=1, device_id=(s + ds, g + dg), device_id_type=MESH)
        pl.when(exists(ds, dg))(signal)
    count = 0
    for ds, dg, _, _ in DIRECTIONS:
        count = count + _step_ok(s, ds, n_sub) * _step_ok(g, dg, n_grp)
    pl.semaphore_wait(barrier, count)

    copies = []
    for j, (k, lo, hi, row) in enumerate(SEND_PIECES):
        ds, dg = DIRECTIONS[k][:2]
        copy = pltpu.make_async_remote_copy(
            src_ref=send_ref.at[:, pl.ds(lo, hi - lo)],
            dst_ref=buf.at[:, pl.ds(row, hi - lo)],
            send_sem=send_sem.at[j],
            recv_sem=recv_sem.at[j],
            device_id=(s + ds, g + dg),
            device_id_type=MESH,
        )
        pl.when(exists(ds, dg))(copy.start)
        copies.append(copy)
    added[...] = jnp.zeros(added.shape, added.dtype)
    for c in range(acc.shape[0]):
        acc[c] = jnp.dot(
            scaled_ref[:, :width], stress_ref[c], precision=lax.Precision.HIGH,
            preferred_element_type=jnp.float32,
        )
    for j, (k, lo, hi, row) in enumerate(SEND_PIECES):
        ds, dg = DIRECTIONS[k][:2]
        pl.when(exists(ds, dg))(copies[j].wait_send)
    for k, (ds, dg, _, _) in enumerate(DIRECTIONS):
        mine = [j for j, piece in enumerate(SEND_PIECES) if piece[0] == k]

        def take(k=k, mine=mine):
            for j in mine:
                copies[j].wait_recv()
            for lo, hi, row in RECV_PIECES[k]:
                added[:, lo:hi, :] += buf[:, row:row + hi - lo, :]

        pl.when(exists(-ds, -dg))(take)
    for c in range(acc.shape[0]):
        total = acc[c] + jnp.dot(
            scaled_ref[:, width:], added[c], precision=lax.Precision.HIGH,
            preferred_element_type=jnp.float32,
        )
        out_ref[c] = total.astype(out_ref.dtype)


def fetch_corners(block, corner_idx, n_sub, n_grp):
    rows, width = block.shape
    slots = 3 * n_grp
    return pl.pallas_call(
        functools.partial(coarse_kernel, n_sub, n_grp),
        out_shape=jax.ShapeDtypeStruct((corner_idx.shape[1], width), block.dtype),
        in_specs=[
            pl.BlockSpec(memory_space=pltpu.VMEM),
            pl.BlockSpec(memory_space=pltpu.SMEM),
        ],
        out_specs=pl.BlockSpec(memory_space=pltpu.VMEM),
        scratch_shapes=[
            pltpu.VMEM((slots * rows, width), block.dtype),
            pltpu.SemaphoreType.DMA((slots,)),
            pltpu.SemaphoreType.DMA((slots,)),
        ],
        compiler_params=pltpu.CompilerParams(collective_id=0, has_side_effects=True),
    )(block, corner_idx)


def exchange_faces(send, stress, scaled, n_sub, n_grp):
    parts, nodes = stress.shape[0], scaled.shape[0]
    return pl.pallas_call(
        functools.partial(face_kernel, n_sub, n_grp),
        out_shape=jax.ShapeDtypeStruct((parts, nodes, send.shape[2]), jnp.bfloat16),
        in_specs=[pl.BlockSpec(memory_space=pltpu.VMEM)] * 3,
        out_specs=pl.BlockSpec(memory_space=pltpu.VMEM),
        scratch_shapes=[
            pltpu.VMEM((send.shape[0], int(SLOT_START[-1]), send.shape[2]), send.dtype),
            pltpu.VMEM(send.shape, send.dtype),
            pltpu.VMEM((parts, nodes, send.shape[2]), jnp.float32),
            pltpu.SemaphoreType.DMA((len(SEND_PIECES),)),
            pltpu.SemaphoreType.DMA((len(SEND_PIECES),)),
        ],
        compiler_params=pltpu.CompilerParams(collective_id=1, has_side_effects=True),
    )(send, stress, scaled)


def shards(
    n_sub,
    n_grp,
    coarse,
    corner_idx,
    coupling,
    force,
    panel_inv,
    panel_nodes,
    strain_disp,
    modulus,
    connect,
    interface,
    nodal_volume,
):
    corner_vals = fetch_corners(coarse, corner_idx, n_sub, n_grp)
    node_count = force.shape[0]
    load_cases = force.shape[2]
    panels = panel_inv.shape[0]
    panel_rows = panel_inv.shape[1]
    correction = jnp.dot(coupling.astype(jnp.float32), corner_vals, precision=lax.Precision.HIGH)
    live_mask = jnp.arange(panel_rows)[None, :] < 3 * panel_nodes[0][:, None]
    reduced = (force.reshape(3 * node_count, load_cases).astype(jnp.float32) - correction).reshape(
        panels, panel_rows, load_cases
    )
    reduced = jnp.where(live_mask[:, :, None], reduced, 0.0).astype(jnp.bfloat16)
    solved = jnp.einsum("prc,pcl->prl", panel_inv, reduced, preferred_element_type=jnp.float32)
    displaced = jnp.where(live_mask[:, :, None], solved, 0.0).astype(jnp.bfloat16)
    by_component = (
        displaced.reshape(panels, panel_rows // 3, 3, load_cases)
        .transpose(2, 0, 1, 3)
        .reshape(3, node_count, load_cases)
    )
    elem_count = connect.shape[1]
    node_range = jnp.arange(node_count, dtype=jnp.int32)
    corner_of = (connect.T.reshape(-1)[:, None] == node_range[None, :]).astype(jnp.bfloat16)
    element = jnp.einsum("xn,cnl->xcl", corner_of, by_component, preferred_element_type=jnp.float32)
    element = element.astype(jnp.bfloat16).reshape(elem_count, 24, load_cases)
    strain = jnp.einsum("ije,ejl->eil", strain_disp, element, preferred_element_type=jnp.float32)
    stress = (
        jnp.einsum("ik,ekl->iel", iso_matrix(), strain, precision=lax.Precision.HIGH)
        * modulus[None, :, None]
    )
    incidence = jnp.sum(
        (connect[:, None, :] == node_range[None, :, None]).astype(jnp.float32), axis=0
    )
    picker = (interface[0][:, None] == node_range[None, :]).astype(jnp.float32)
    send = jnp.einsum(
        "re,cel->crl", jnp.dot(picker, incidence), stress, precision=lax.Precision.HIGH
    )
    inverse_volume = 1.0 / nodal_volume
    scaled = jnp.concatenate([incidence, picker.T], axis=1) * inverse_volume[:, None]
    stress_out = exchange_faces(send, stress, scaled, n_sub, n_grp).transpose(1, 0, 2)
    return (by_component.transpose(1, 0, 2), stress_out)


def solution(mesh):
    n_sub = mesh.shape["sub"]
    n_grp = mesh.shape["grp"]
    placed = (
        P(("sub", "grp"), None),
        P(("sub", "grp"), None),
        P(("sub", "grp"), None),
        P(("sub", "grp"), None, None),
        P(("sub", "grp"), None, None),
        P(("sub", "grp"), None),
        P(None, None, ("sub", "grp")),
        P(("sub", "grp")),
        P(None, ("sub", "grp")),
        P(("sub", "grp"), None),
        P(("sub", "grp")),
    )
    return jax.shard_map(
        functools.partial(shards, n_sub, n_grp),
        mesh=mesh,
        in_specs=placed,
        out_specs=(P(("sub", "grp"), None, None), P(("sub", "grp"), None, None)),
        check_vma=False,
    )
```
